32 devices in a mesh: spec: 8 (over z, y), wave: 4 (over x, core).
Axes of the slice: x: 2, y: 2, z: 4, core: 2. Of those that a mesh axis runs over, the one named last changes fastest.
Arguments:
- observed_flux: bfloat16 [2048, 2048], P('spec', 'wave'), may hold values from -6 to 6
- continuum_coeffs: bfloat16 [2048, 16], P('spec'), may hold values from -6 to 6
- continuum_basis: bfloat16 [16, 2048], P(None, 'wave'), may hold values from -1.5 to 1.5
- centres: int32 [2048, 16], P('spec', 'wave'), may hold values from 0 to 2047, as said below
- line_index: int32 [2048, 16], P('spec', 'wave'), may hold values from 0 to 31
- column_factor: float32 [2048, 16], P('spec', 'wave'), may hold values from 0.3 to 3
- wing_width: int32 [2048], P('spec'), may hold values from 8 to 32, as said below
- line_strength: float32 [32], replicated, may hold values from 0.2 to 2
- line_widths: float32 [32], replicated, may hold values from 1 to 6
- sketch_matrix: bfloat16 [2048, 512], P('wave'), may hold values from -0.125 to 0.125
Outputs:
- residual: bfloat16 [2048, 2048], P('spec', 'wave')
- rfactor: float32 [512, 512], replicated
The draws below stay inside these ranges and needn't reach their ends.
Inputs may be any that keep to these rules, and one draw needn't show every extreme that they name: The absorbers in columns k * 4 to (k + 1) * 4 - 1 have centres in pixels k * 512 to (k + 1) * 512 - 1; spectrum 0 has absorbers at pixel 0 and at pixel 2048 - 1. `wing_width`: spectrum 0 has the largest half-width.
All inputs are finite; a program needn't handle non-finite values.
Results may differ from the reference program's by a relative error of at most 0.0026.
Values sent between devices are 32-bit elements; how exact they have to be, the bound alone decides.
No kernel may reach another device: no remote copies, remote signals or barrier semaphores. Data moves between devices by JAX's collectives and lax.ppermute only.
A program may use at most 64 MiB of HBM per device.

```python
import math
import jax
import jax.numpy as jnp
from jax import lax

SPEC_DEV = 256
PIX_DEV = 512
K = 512
A_DEV = 4
NLINES = 32
NBASIS = 16
WING = 32
SPECTRA = 2048
PIX = 2048
ABSORBERS = 16


def draw_centres(key, part):
    block = jnp.arange(ABSORBERS, dtype=jnp.int32) // A_DEV
    offset = jax.random.randint(key, (SPECTRA, ABSORBERS), 0, PIX_DEV, dtype=jnp.int32)
    placed = block[None, :] * PIX_DEV + offset
    return placed.at[0, 0].set(0).at[0, ABSORBERS - 1].set(PIX - 1)


def draw_wing_width(key, part):
    widths = jax.random.randint(key, (SPECTRA,), WING // 4, WING + 1, dtype=jnp.int32)
    return widths.at[0].set(WING)


def place_ends(values, key, least, largest):
    spot = [jax.random.randint(jax.random.fold_in(key, axis), (), 0, length) for axis, length in enumerate(values.shape)]
    main_axis = values.shape.index(max(values.shape))
    neighbour = spot[:main_axis] + [(spot[main_axis] + 1) % values.shape[main_axis]] + spot[main_axis + 1:]
    return values.at[tuple(spot)].set(least).at[tuple(neighbour)].set(largest)


def block_levels(key, shape, pieces, smallest, high):
    def one(axis_at, blocks):
        steps = jax.random.uniform(jax.random.fold_in(jax.random.fold_in(key, 6), axis_at), (blocks,), jnp.float32, smallest / len(pieces), high / len(pieces))
        return jnp.repeat(jnp.exp(steps), shape[axis_at] // blocks).reshape((-1,) + (1,) * (len(shape) - axis_at - 1))

    level = one(*pieces[0])
    for cut in pieces[1:]:
        level = level * one(*cut)
    return level


def bell_draw(rng, shape, spread, reach, shards=(), kind=jnp.bfloat16):
    drawn = jax.random.normal(rng, shape, jnp.float32) * spread
    if len(shards) > 0:
        drawn = block_levels(rng, shape, shards, -0.22, 0.18) * drawn
    return jnp.clip(drawn, min=-reach, max=reach).astype(kind)


def setup_inputs(seed: int = 0) -> dict:
    arg_keys = jax.random.split(jax.random.key(seed), 11)
    observed_flux = bell_draw(arg_keys[0], (SPECTRA, PIX), 1.0, 6.0, ((0, 8), (1, 4)))
    continuum_coeffs = bell_draw(arg_keys[1], (SPECTRA, NBASIS), 1.0, 6.0, ((0, 8),))
    continuum_basis = bell_draw(arg_keys[2], (NBASIS, PIX), NBASIS ** -0.5, 1.5, ((1, 4),))
    centres = draw_centres(jax.random.fold_in(arg_keys[10], 71), 0)
    line_index = place_ends(jax.random.randint(arg_keys[4], (SPECTRA, ABSORBERS), 0, NLINES), jax.random.fold_in(arg_keys[4], 1), 0, NLINES - 1).astype(jnp.int32)
    column_factor = jnp.clip(jnp.exp(math.log(3.0) - 2.3025851 * jax.random.uniform(arg_keys[5], (SPECTRA, ABSORBERS), jnp.float32) ** block_levels(arg_keys[5], (SPECTRA, ABSORBERS), ((0, 8), (1, 4)), -0.2, 0.2)), 0.3, 3.0)
    wing_width = draw_wing_width(jax.random.fold_in(arg_keys[10], 71), 0)
    line_strength = jnp.clip(jnp.exp(jax.random.uniform(arg_keys[7], (NLINES,), jnp.float32, math.log(0.2), math.log(2.0))), 0.2, 2.0)
    line_widths = jnp.clip(jnp.exp(jax.random.uniform(arg_keys[8], (NLINES,), jnp.float32, math.log(1.0), math.log(6.0))), 1.0, 6.0)
    sketch_matrix = bell_draw(arg_keys[9], (PIX, K), PIX ** -0.5, 0.125, ((0, 4),))
    return dict(observed_flux=observed_flux, continuum_coeffs=continuum_coeffs, continuum_basis=continuum_basis, centres=centres, line_index=line_index, column_factor=column_factor, wing_width=wing_width, line_strength=line_strength, line_widths=line_widths, sketch_matrix=sketch_matrix)


voigt_mix = 0.5
log_two = 0.6931471805599453

def profile(offset, amplitude, inverse_width, wing_limit):
    scaled = offset * inverse_width
    values = amplitude * (voigt_mix / (1.0 + scaled * scaled) + (1.0 - voigt_mix) * jnp.exp(-log_two * scaled * scaled))
    return jnp.where(jnp.abs(offset) <= wing_limit, values, 0.0)

def block_terms(inputs, continuum_basis, line_strength, line_widths, sketch_matrix):
    flux_block, coeff_block, centre_block, line_block, column_block, wing_block = inputs
    onehot = (line_block[:, :, None] == jnp.arange(NLINES, dtype=jnp.int32)[None, None, :]).astype(jnp.float32)
    amplitude = column_block * jnp.sum(onehot * line_strength, axis=2)
    inverse_width = 1.0 / jnp.sum(onehot * line_widths, axis=2)
    offsets = jnp.arange(-WING, WING + 1, dtype=jnp.int32)
    offset_float = jnp.broadcast_to(offsets.astype(jnp.float32)[None, None, :], centre_block.shape + (2 * WING + 1,))
    values = profile(offset_float, amplitude[:, :, None], inverse_width[:, :, None], wing_block.astype(jnp.float32)[:, None, None])
    columns = (centre_block[:, :, None] + offsets[None, None, :] + WING).astype(jnp.int32)
    row_ids = jnp.broadcast_to(jnp.arange(centre_block.shape[0], dtype=jnp.int32)[:, None, None], columns.shape)
    padded = jnp.zeros((centre_block.shape[0], PIX + 2 * WING), jnp.float32).at[row_ids, columns].add(values)
    optical_depth = padded[:, WING:WING + PIX]
    continuum = jnp.dot(coeff_block.astype(jnp.float32), continuum_basis.astype(jnp.float32), preferred_element_type=jnp.float32)
    residual = (flux_block.astype(jnp.float32) - continuum * jnp.exp(-optical_depth)).astype(jnp.bfloat16)
    sketch = jnp.dot(residual.astype(jnp.float32), sketch_matrix.astype(jnp.float32), preferred_element_type=jnp.float32)
    return (residual, sketch)

def reference(observed_flux, continuum_coeffs, continuum_basis, centres, line_index, column_factor, wing_width, line_strength, line_widths, sketch_matrix):
    count = SPECTRA // SPEC_DEV
    inputs = (observed_flux.reshape(count, SPEC_DEV, PIX), continuum_coeffs.reshape(count, SPEC_DEV, NBASIS), centres.reshape(count, SPEC_DEV, ABSORBERS), line_index.reshape(count, SPEC_DEV, ABSORBERS), column_factor.reshape(count, SPEC_DEV, ABSORBERS), wing_width.reshape(count, SPEC_DEV))
    residual, sketch = lax.map(lambda item: block_terms(item, continuum_basis, line_strength, line_widths, sketch_matrix), inputs)
    residual = residual.reshape(SPECTRA, PIX)
    sketch = sketch.reshape(SPECTRA, K)
    gram_matrix = jnp.dot(sketch.T.astype(jnp.float32), sketch.astype(jnp.float32), precision=lax.Precision.HIGHEST, preferred_element_type=jnp.float32) / SPECTRA
    rfactor = jnp.linalg.cholesky(gram_matrix).T
    return (residual, rfactor)
```

```python
import jax
import jax.numpy as jnp
from jax import lax
from jax.experimental import pallas as pl
from jax.experimental.pallas import tpu as pltpu
from jax.sharding import PartitionSpec as P

WING = 32
T = 128
S = 8
HI = lax.Precision.HIGHEST

def rows_of(x, k):
    return jnp.broadcast_to(x[k:k + 1, :], x.shape)

def lanes_of(x, c):
    return jnp.broadcast_to(x[:, c:c + 1], x.shape)

def factor_block(d_ref, rk_ref, x_ref):
    steps = T // S
    sub = lax.broadcasted_iota(jnp.int32, (S, T), 0)
    lane = lax.broadcasted_iota(jnp.int32, (S, T), 1)
    at = [sub == k for k in range(S)]
    D = [d_ref[S * g:S * g + S, 0:T] for g in range(steps)]
    E = [jnp.where(lane == sub + S * g, 1.0, 0.0).astype(jnp.float32) for g in range(steps)]
    C = [lanes_of(D[0], k) for k in range(S)]
    for s in range(steps):
        Z = [rows_of(D[s], k) for k in range(S)]
        Y = [rows_of(E[s], k) for k in range(S)]
        B = Cn = None
        if s + 1 < steps:
            B = [lanes_of(D[s + 1], S * s + k) for k in range(S)]
            Cn = [lanes_of(D[s + 1], S * (s + 1) + k) for k in range(S)]
        for k in range(S):
            d = rows_of(C[k], k)
            inv = 1.0 / d
            rs = lax.rsqrt(d)
            rk_ref[S * s + k:S * s + k + 1, :] = (Z[k] * rs)[0:1]
            x_ref[S * s + k:S * s + k + 1, :] = (Y[k] * rs)[0:1]
            Z[k] = Z[k] * inv
            Y[k] = Y[k] * inv
            u = {}
            for c in range(k + 1, S):
                u[c] = rows_of(C[c], k) * inv
                C[c] = jnp.where(at[k], u[c], C[c] - C[k] * u[c])
            for c in range(S):
                if c != k:
                    m = rows_of(C[k], c)
                    Z[c] = Z[c] - m * Z[k]
                    Y[c] = Y[c] - m * Y[k]
            if B is not None:
                bi = B[k] * inv
                for c in range(k + 1, S):
                    B[c] = B[c] - B[k] * u[c]
                for c in range(S):
                    Cn[c] = Cn[c] - bi * rows_of(B[k], c)
        for g in range(s + 1, steps):
            raw = [lanes_of(D[g], S * s + k) for k in range(S)]
            dd, ee = D[g], E[g]
            for k in range(S):
                dd = dd - raw[k] * Z[k]
                ee = ee - raw[k] * Y[k]
            D[g], E[g] = dd, ee
        C = Cn

def chol_body(a_ref, r_ref, w_ref, rk_ref, x_ref):
    n = a_ref.shape[0]
    nb = n // T
    w_ref[...] = a_ref[...]
    r_ref[...] = jnp.zeros_like(r_ref)
    row = lax.broadcasted_iota(jnp.int32, (T, T), 0)
    col = lax.broadcasted_iota(jnp.int32, (T, T), 1)
    def step(b, _):
        factor_block(w_ref, rk_ref, x_ref)
        base = pl.multiple_of(b * T, T)
        r_ref[pl.ds(base, T), pl.ds(base, T)] = jnp.where(row <= col, rk_ref[...], 0.0)
        @pl.when(b < nb - 1)
        def _():
            x = jnp.where(row >= col, x_ref[...], 0.0)
            panel = jnp.dot(x, w_ref[0:T, T:n], precision=HI, preferred_element_type=jnp.float32)
            for t in range(nb - 1):
                @pl.when(b + 1 + t < nb)
                def _():
                    r_ref[pl.ds(base, T), pl.ds(pl.multiple_of(base + (t + 1) * T, T), T)] = panel[:, t * T:(t + 1) * T]
            for i in range(nb - 1):
                left = panel[:, i * T:(i + 1) * T]
                right = panel[:, i * T:]
                upd = lax.dot_general(left, right, (((0,), (0,)), ((), ())), precision=HI, preferred_element_type=jnp.float32)
                w_ref[i * T:(i + 1) * T, i * T:n - T] = w_ref[(i + 1) * T:(i + 2) * T, (i + 1) * T:n] - upd
        return 0
    lax.fori_loop(0, nb, step, 0)

def chol(a):
    n = a.shape[0]
    return pl.pallas_call(
        chol_body, name="factor",
        out_shape=jax.ShapeDtypeStruct((n, n), jnp.float32),
        scratch_shapes=[pltpu.VMEM((n, n), jnp.float32), pltpu.VMEM((T, T), jnp.float32), pltpu.VMEM((T, T), jnp.float32)],
        compiler_params=pltpu.CompilerParams(vmem_limit_bytes=32 << 20),
    )(a)


voigt_mix = 0.5
log_two = 0.6931471805599453


def extended_2(block, sides, width):
    for axis, dim in sides:
        count = lax.axis_size(axis)
        forward = [(i, i + 1) for i in range(count - 1)]
        backward = [(target, source) for source, target in forward]
        low = lax.ppermute(
            lax.slice_in_dim(block, block.shape[dim] - width, None, axis=dim), axis, forward
        )
        high = lax.ppermute(lax.slice_in_dim(block, 0, width, axis=dim), axis, backward)
        block = jnp.concatenate([low, block, high], axis=dim)
    return block


def profile(offset, amplitude, inverse_width, wing_limit):
    scaled = offset * inverse_width
    values = amplitude * (
        voigt_mix / (1.0 + scaled * scaled)
        + (1.0 - voigt_mix) * jnp.exp(-log_two * scaled * scaled)
    )
    return jnp.where(jnp.abs(offset) <= wing_limit, values, 0.0)


def windowed_depth(centre_int, amplitude, inverse_width, wing_limit, anchor, width):
    pixels = anchor + jnp.arange(width, dtype=jnp.int32)
    offset_int = pixels[None, None, :] - centre_int[:, :, None]
    offset_float = offset_int.astype(jnp.float32)
    values = profile(
        offset_float, amplitude[:, :, None], inverse_width[:, :, None], wing_limit[:, :, None]
    )
    return jnp.sum(values, axis=1)


def shards(
    observed_flux,
    continuum_coeffs,
    continuum_basis,
    centres,
    line_index,
    column_factor,
    wing_width,
    line_strength,
    line_widths,
    sketch_matrix,
):
    spectra, pix_local = observed_flux.shape
    first_pixel = lax.axis_index("wave") * pix_local
    onehot = (
        line_index[:, :, None] == jnp.arange(line_strength.shape[0], dtype=jnp.int32)[None, None, :]
    ).astype(jnp.float32)
    amplitude = column_factor * jnp.sum(onehot * line_strength, axis=2)
    inverse_width = 1.0 / jnp.sum(onehot * line_widths, axis=2)
    wing_limit = wing_width.astype(jnp.float32)[:, None]
    extended = windowed_depth(
        centres, amplitude, inverse_width, wing_limit, first_pixel - WING, pix_local + 2 * WING
    )
    outgoing = jnp.concatenate([extended[:, :WING], extended[:, -WING:]], axis=1)
    padded_rims = extended_2(outgoing, (("wave", 1),), WING)
    optical_depth = extended[:, WING:-WING]
    optical_depth = optical_depth.at[:, :WING].add(padded_rims[:, :WING])
    optical_depth = optical_depth.at[:, -WING:].add(padded_rims[:, 3 * WING :])
    continuum = jnp.dot(continuum_coeffs, continuum_basis, preferred_element_type=jnp.float32)
    residual = (observed_flux.astype(jnp.float32) - continuum * jnp.exp(-optical_depth)).astype(
        jnp.bfloat16
    )
    spectra_total = spectra * lax.axis_size("spec")
    partial_sketch = jnp.dot(residual, sketch_matrix, preferred_element_type=jnp.float32)
    sketch = lax.psum(partial_sketch, "wave")
    local_gram = jnp.dot(
        sketch.T, sketch, precision=lax.Precision.HIGHEST, preferred_element_type=jnp.float32
    )
    gram_matrix = lax.psum(local_gram, "spec")
    gram_matrix = gram_matrix / spectra_total
    rfactor = chol(gram_matrix)
    return (residual, rfactor)


def solution(mesh):
    return jax.shard_map(
        shards,
        mesh=mesh,
        in_specs=(
            P("spec", "wave"),
            P("spec", None),
            P(None, "wave"),
            P("spec", "wave"),
            P("spec", "wave"),
            P("spec", "wave"),
            P("spec"),
            P(),
            P(),
            P("wave", None),
        ),
        out_specs=(P("spec", "wave"), P()),
        check_vma=False,
    )
```

```python
import jax
import jax.numpy as jnp
from jax import lax
from jax.experimental import pallas as pl
from jax.experimental.pallas import tpu as pltpu
from jax.sharding import PartitionSpec as P

WING = 32
T = 128
S = 8
HI = lax.Precision.HIGHEST

def rows_of(x, k):
    return jnp.broadcast_to(x[k:k + 1, :], x.shape)

def lanes_of(x, c):
    return jnp.broadcast_to(x[:, c:c + 1], x.shape)

def factor_block(d_ref, rk_ref, x_ref):
    steps = T // S
    sub = lax.broadcasted_iota(jnp.int32, (S, T), 0)
    lane = lax.broadcasted_iota(jnp.int32, (S, T), 1)
    at = [sub == k for k in range(S)]
    D = [d_ref[S * g:S * g + S, 0:T] for g in range(steps)]
    E = [jnp.where(lane == sub + S * g, 1.0, 0.0).astype(jnp.float32) for g in range(steps)]
    C = [lanes_of(D[0], k) for k in range(S)]
    for s in range(steps):
        Z = [rows_of(D[s], k) for k in range(S)]
        Y = [rows_of(E[s], k) for k in range(S)]
        B = Cn = None
        if s + 1 < steps:
            B = [lanes_of(D[s + 1], S * s + k) for k in range(S)]
            Cn = [lanes_of(D[s + 1], S * (s + 1) + k) for k in range(S)]
        for k in range(S):
            d = rows_of(C[k], k)
            inv = 1.0 / d
            rs = lax.rsqrt(d)
            rk_ref[S * s + k:S * s + k + 1, :] = (Z[k] * rs)[0:1]
            x_ref[S * s + k:S * s + k + 1, :] = (Y[k] * rs)[0:1]
            Z[k] = Z[k] * inv
            Y[k] = Y[k] * inv
            u = {}
            for c in range(k + 1, S):
                u[c] = rows_of(C[c], k) * inv
                C[c] = jnp.where(at[k], u[c], C[c] - C[k] * u[c])
            for c in range(S):
                if c != k:
                    m = rows_of(C[k], c)
                    Z[c] = Z[c] - m * Z[k]
                    Y[c] = Y[c] - m * Y[k]
            if B is not None:
                bi = B[k] * inv
                for c in range(k + 1, S):
                    B[c] = B[c] - B[k] * u[c]
                for c in range(S):
                    Cn[c] = Cn[c] - bi * rows_of(B[k], c)
        for g in range(s + 1, steps):
            raw = [lanes_of(D[g], S * s + k) for k in range(S)]
            dd, ee = D[g], E[g]
            for k in range(S):
                dd = dd - raw[k] * Z[k]
                ee = ee - raw[k] * Y[k]
            D[g], E[g] = dd, ee
        C = Cn

def upper_block(b, nb):
    i = jnp.int32(0)
    start = jnp.int32(0)
    for r in range(1, nb):
        first = r * nb - r * (r - 1) // 2
        i = i + (b >= first).astype(jnp.int32)
        start = jnp.where(b >= first, first, start)
    return i, i + b - start


def blocks_of(x, slots, t, nb):
    b = jnp.minimum(x * slots + t, nb * (nb + 1) // 2 - 1)
    i, j = upper_block(b, nb)
    return pl.multiple_of(i * T, T), pl.multiple_of(j * T, T)


def gram_blocks(mine, other, slots, scale):
    rows, k = mine.shape

    def body(mine_ref, other_ref, keep_ref, send_ref, s_ref, g_ref):
        w = lax.axis_index("wave")
        core, x = w % 2, w // 2
        s_ref[...] = mine_ref[...] + other_ref[...]
        for t in range(slots):
            i, j = blocks_of(x, slots, t, k // T)
            g_ref[...] = scale * lax.dot_general(
                s_ref[:, pl.ds(i, T)], s_ref[:, pl.ds(j, T)], (((0,), (0,)), ((), ())),
                precision=HI, preferred_element_type=jnp.float32)
            half = T // 2
            keep_ref[t] = g_ref[pl.ds(pl.multiple_of(core * half, half), half), :]
            send_ref[t] = g_ref[pl.ds(pl.multiple_of((1 - core) * half, half), half), :]

    shape = jax.ShapeDtypeStruct((slots, T // 2, T), jnp.float32)
    return pl.pallas_call(
        body, name="gram", out_shape=(shape, shape),
        scratch_shapes=[pltpu.VMEM((rows, k), jnp.float32), pltpu.VMEM((T, T), jnp.float32)],
        compiler_params=pltpu.CompilerParams(vmem_limit_bytes=32 << 20),
    )(mine, other)


def factor(pieces, offsets, slots, n):
    nb = n // T
    part = T // 4

    def body(*refs):
        piece_refs, (r_ref, w_ref, rk_ref, x_ref) = refs[:len(pieces)], refs[len(pieces):]
        w = lax.axis_index("wave")
        y = lax.axis_index("spec") % 2
        for ref, (dw, dy) in zip(piece_refs, offsets):
            v = w ^ dw
            core, x = v % 2, v // 2
            row = pl.multiple_of(core * (T // 2) + (y ^ dy) * part, part)
            for t in range(slots):
                i, j = blocks_of(x, slots, t, nb)
                w_ref[pl.ds(pl.multiple_of(i + row, part), part), pl.ds(j, T)] = ref[t]
        r_ref[...] = jnp.zeros_like(r_ref)
        row = lax.broadcasted_iota(jnp.int32, (T, T), 0)
        col = lax.broadcasted_iota(jnp.int32, (T, T), 1)

        def step(b, _):
            factor_block(w_ref, rk_ref, x_ref)
            base = pl.multiple_of(b * T, T)
            r_ref[pl.ds(base, T), pl.ds(base, T)] = jnp.where(row <= col, rk_ref[...], 0.0)

            @pl.when(b < nb - 1)
            def _():
                x = jnp.where(row >= col, x_ref[...], 0.0)
                panel = jnp.dot(x, w_ref[0:T, T:n], precision=HI, preferred_element_type=jnp.float32)
                for t in range(nb - 1):
                    @pl.when(b + 1 + t < nb)
                    def _():
                        at = pl.multiple_of(base + (t + 1) * T, T)
                        r_ref[pl.ds(base, T), pl.ds(at, T)] = panel[:, t * T:(t + 1) * T]
                for i in range(nb - 1):
                    update = lax.dot_general(
                        panel[:, i * T:(i + 1) * T], panel[:, i * T:], (((0,), (0,)), ((), ())),
                        precision=HI, preferred_element_type=jnp.float32)
                    w_ref[i * T:(i + 1) * T, i * T:n - T] = w_ref[(i + 1) * T:(i + 2) * T, (i + 1) * T:n] - update
            return 0

        lax.fori_loop(0, nb, step, 0)

    return pl.pallas_call(
        body, name="factor", out_shape=jax.ShapeDtypeStruct((n, n), jnp.float32),
        scratch_shapes=[pltpu.VMEM((n, n), jnp.float32), pltpu.VMEM((T, T), jnp.float32),
                        pltpu.VMEM((T, T), jnp.float32)],
        compiler_params=pltpu.CompilerParams(vmem_limit_bytes=32 << 20),
    )(*pieces)


def swap(x, axis, bit):
    return lax.ppermute(x, axis, [(i, i ^ bit) for i in range(lax.axis_size(axis))])


def bits_from(first, count):
    bits = []
    while first < count:
        bits.append(first)
        first *= 2
    return bits


def half_of(x, which, dim):
    size = x.shape[dim] // 2
    return lax.dynamic_slice_in_dim(x, which * size, size, dim)


def reduce_and_factor(partial_sketch, spectra_total):
    waves, specs = lax.axis_size("wave"), lax.axis_size("spec")
    core, y = lax.axis_index("wave") % 2, lax.axis_index("spec") % 2
    k = partial_sketch.shape[1]
    slots = -(-((k // T) * (k // T + 1) // 2) // (waves // 2))
    mine = half_of(partial_sketch, core, 0)
    other = swap(half_of(partial_sketch, 1 - core, 0), "wave", 1)
    for bit in bits_from(2, waves):
        mine = mine + other
        other = swap(mine, "wave", bit)
    keep, send = gram_blocks(mine, other, slots, 1.0 / spectra_total)
    got = swap(send, "wave", 1)
    mine = half_of(keep, y, 1) + half_of(got, y, 1)
    other = half_of(keep, 1 - y, 1) + half_of(got, 1 - y, 1)
    mine = mine + swap(other, "spec", 1)
    for bit in bits_from(2, specs):
        mine = mine + swap(mine, "spec", bit)
    pieces, offsets = [mine], [(0, 0)]
    steps = [("spec", 1)] + [("wave", b) for b in bits_from(2, waves)] + [("wave", 1)]
    for axis, bit in steps:
        pieces = pieces + [swap(p, axis, bit) for p in pieces]
        offsets = offsets + [(w ^ (bit if axis == "wave" else 0), y_ ^ (bit if axis == "spec" else 0)) for w, y_ in offsets]
    return factor(pieces, offsets, slots, k)


voigt_mix = 0.5
log_two = 0.6931471805599453


def extended_2(block, sides, width):
    for axis, dim in sides:
        count = lax.axis_size(axis)
        forward = [(i, i + 1) for i in range(count - 1)]
        backward = [(target, source) for source, target in forward]
        low = lax.ppermute(
            lax.slice_in_dim(block, block.shape[dim] - width, None, axis=dim), axis, forward
        )
        high = lax.ppermute(lax.slice_in_dim(block, 0, width, axis=dim), axis, backward)
        block = jnp.concatenate([low, block, high], axis=dim)
    return block


def profile(offset, amplitude, inverse_width, wing_limit):
    scaled = offset * inverse_width
    values = amplitude * (
        voigt_mix / (1.0 + scaled * scaled)
        + (1.0 - voigt_mix) * jnp.exp(-log_two * scaled * scaled)
    )
    return jnp.where(jnp.abs(offset) <= wing_limit, values, 0.0)


def windowed_depth(centre_int, amplitude, inverse_width, wing_limit, anchor, width):
    pixels = anchor + jnp.arange(width, dtype=jnp.int32)
    offset_int = pixels[None, None, :] - centre_int[:, :, None]
    offset_float = offset_int.astype(jnp.float32)
    values = profile(
        offset_float, amplitude[:, :, None], inverse_width[:, :, None], wing_limit[:, :, None]
    )
    return jnp.sum(values, axis=1)


def shards(
    observed_flux,
    continuum_coeffs,
    continuum_basis,
    centres,
    line_index,
    column_factor,
    wing_width,
    line_strength,
    line_widths,
    sketch_matrix,
):
    spectra, pix_local = observed_flux.shape
    first_pixel = lax.axis_index("wave") * pix_local
    onehot = (
        line_index[:, :, None] == jnp.arange(line_strength.shape[0], dtype=jnp.int32)[None, None, :]
    ).astype(jnp.float32)
    amplitude = column_factor * jnp.sum(onehot * line_strength, axis=2)
    inverse_width = 1.0 / jnp.sum(onehot * line_widths, axis=2)
    wing_limit = wing_width.astype(jnp.float32)[:, None]
    extended = windowed_depth(
        centres, amplitude, inverse_width, wing_limit, first_pixel - WING, pix_local + 2 * WING
    )
    outgoing = jnp.concatenate([extended[:, :WING], extended[:, -WING:]], axis=1)
    padded_rims = extended_2(outgoing, (("wave", 1),), WING)
    optical_depth = extended[:, WING:-WING]
    optical_depth = optical_depth.at[:, :WING].add(padded_rims[:, :WING])
    optical_depth = optical_depth.at[:, -WING:].add(padded_rims[:, 3 * WING :])
    continuum = jnp.dot(continuum_coeffs, continuum_basis, preferred_element_type=jnp.float32)
    residual = (observed_flux.astype(jnp.float32) - continuum * jnp.exp(-optical_depth)).astype(
        jnp.bfloat16
    )
    spectra_total = spectra * lax.axis_size("spec")
    partial_sketch = jnp.dot(residual, sketch_matrix, preferred_element_type=jnp.float32)
    rfactor = reduce_and_factor(partial_sketch, spectra_total)
    return (residual, rfactor)


def solution(mesh):
    return jax.shard_map(
        shards,
        mesh=mesh,
        in_specs=(
            P("spec", "wave"),
            P("spec", None),
            P(None, "wave"),
            P("spec", "wave"),
            P("spec", "wave"),
            P("spec", "wave"),
            P("spec"),
            P(),
            P(),
            P("wave", None),
        ),
        out_specs=(P("spec", "wave"), P()),
        check_vma=False,
    )
```

```python
import jax
import jax.numpy as jnp
from jax import lax
from jax.experimental import pallas as pl
from jax.experimental.pallas import tpu as pltpu
from jax.sharding import PartitionSpec as P

WING = 32
T = 128
S = 8
HI = lax.Precision.HIGHEST

def rows_of(x, k):
    return jnp.broadcast_to(x[k:k + 1, :], x.shape)

def lanes_of(x, c):
    return jnp.broadcast_to(x[:, c:c + 1], x.shape)

def factor_block(d_ref, rk_ref, x_ref):
    steps = T // S
    sub = lax.broadcasted_iota(jnp.int32, (S, T), 0)
    lane = lax.broadcasted_iota(jnp.int32, (S, T), 1)
    at = [sub == k for k in range(S)]
    D = [d_ref[S * g:S * g + S, 0:T] for g in range(steps)]
    E = [jnp.where(lane == sub + S * g, 1.0, 0.0).astype(jnp.float32) for g in range(steps)]
    C = [lanes_of(D[0], k) for k in range(S)]
    for s in range(steps):
        Z = [rows_of(D[s], k) for k in range(S)]
        Y = [rows_of(E[s], k) for k in range(S)]
        B = Cn = None
        if s + 1 < steps:
            B = [lanes_of(D[s + 1], S * s + k) for k in range(S)]
            Cn = [lanes_of(D[s + 1], S * (s + 1) + k) for k in range(S)]
        for k in range(S):
            d = rows_of(C[k], k)
            inv = 1.0 / d
            rs = lax.rsqrt(d)
            rk_ref[S * s + k:S * s + k + 1, :] = (Z[k] * rs)[0:1]
            x_ref[S * s + k:S * s + k + 1, :] = (Y[k] * rs)[0:1]
            Z[k] = Z[k] * inv
            Y[k] = Y[k] * inv
            u = {}
            for c in range(k + 1, S):
                u[c] = rows_of(C[c], k) * inv
                C[c] = jnp.where(at[k], u[c], C[c] - C[k] * u[c])
            for c in range(S):
                if c != k:
                    m = rows_of(C[k], c)
                    Z[c] = Z[c] - m * Z[k]
                    Y[c] = Y[c] - m * Y[k]
            if B is not None:
                bi = B[k] * inv
                for c in range(k + 1, S):
                    B[c] = B[c] - B[k] * u[c]
                for c in range(S):
                    Cn[c] = Cn[c] - bi * rows_of(B[k], c)
        for g in range(s + 1, steps):
            raw = [lanes_of(D[g], S * s + k) for k in range(S)]
            dd, ee = D[g], E[g]
            for k in range(S):
                dd = dd - raw[k] * Z[k]
                ee = ee - raw[k] * Y[k]
            D[g], E[g] = dd, ee
        C = Cn

def upper_block(b, nb):
    i = jnp.int32(0)
    start = jnp.int32(0)
    for r in range(1, nb):
        first = r * nb - r * (r - 1) // 2
        i = i + (b >= first).astype(jnp.int32)
        start = jnp.where(b >= first, first, start)
    return i, i + b - start


def blocks_of(x, slots, t, nb):
    b = jnp.minimum(x * slots + t, nb * (nb + 1) // 2 - 1)
    i, j = upper_block(b, nb)
    return pl.multiple_of(i * T, T), pl.multiple_of(j * T, T)


def gram_blocks(mine, other, slots, scale):
    rows, k = mine.shape

    def body(mine_ref, other_ref, keep_ref, send_ref, s_ref, g_ref):
        w = lax.axis_index("wave")
        core, x = w % 2, w // 2
        s_ref[...] = mine_ref[...] + other_ref[...]
        for t in range(slots):
            i, j = blocks_of(x, slots, t, k // T)
            g_ref[...] = scale * lax.dot_general(
                s_ref[:, pl.ds(i, T)], s_ref[:, pl.ds(j, T)], (((0,), (0,)), ((), ())),
                precision=HI, preferred_element_type=jnp.float32)
            half = T // 2
            keep_ref[t] = g_ref[pl.ds(pl.multiple_of(core * half, half), half), :]
            send_ref[t] = g_ref[pl.ds(pl.multiple_of((1 - core) * half, half), half), :]

    shape = jax.ShapeDtypeStruct((slots, T // 2, T), jnp.float32)
    return pl.pallas_call(
        body, name="gram", out_shape=(shape, shape),
        scratch_shapes=[pltpu.VMEM((rows, k), jnp.float32), pltpu.VMEM((T, T), jnp.float32)],
        compiler_params=pltpu.CompilerParams(vmem_limit_bytes=32 << 20),
    )(mine, other)


def factor(pieces, offsets, slots, n):
    nb = n // T
    part = T // 4

    def body(*refs):
        piece_refs, (r_ref, w_ref, rk_ref, x_ref) = refs[:len(pieces)], refs[len(pieces):]
        w = lax.axis_index("wave")
        y = lax.axis_index("spec") % 2
        for ref, (dw, dy) in zip(piece_refs, offsets):
            v = w ^ dw
            core, x = v % 2, v // 2
            row = pl.multiple_of(core * (T // 2) + (y ^ dy) * part, part)
            for t in range(slots):
                i, j = blocks_of(x, slots, t, nb)
                w_ref[pl.ds(pl.multiple_of(i + row, part), part), pl.ds(j, T)] = ref[t]
        r_ref[...] = jnp.zeros_like(r_ref)
        row = lax.broadcasted_iota(jnp.int32, (T, T), 0)
        col = lax.broadcasted_iota(jnp.int32, (T, T), 1)

        def step(b, _):
            factor_block(w_ref, rk_ref, x_ref)
            base = pl.multiple_of(b * T, T)
            r_ref[pl.ds(base, T), pl.ds(base, T)] = jnp.where(row <= col, rk_ref[...], 0.0)

            @pl.when(b < nb - 1)
            def _():
                x = jnp.where(row >= col, x_ref[...], 0.0)
                panel = jnp.dot(x, w_ref[0:T, T:n], precision=HI, preferred_element_type=jnp.float32)
                for t in range(nb - 1):
                    @pl.when(b + 1 + t < nb)
                    def _():
                        at = pl.multiple_of(base + (t + 1) * T, T)
                        r_ref[pl.ds(base, T), pl.ds(at, T)] = panel[:, t * T:(t + 1) * T]
                for i in range(nb - 1):
                    update = lax.dot_general(
                        panel[:, i * T:(i + 1) * T], panel[:, i * T:], (((0,), (0,)), ((), ())),
                        precision=HI, preferred_element_type=jnp.float32)
                    w_ref[i * T:(i + 1) * T, i * T:n - T] = w_ref[(i + 1) * T:(i + 2) * T, (i + 1) * T:n] - update
            return 0

        lax.fori_loop(0, nb, step, 0)

    return pl.pallas_call(
        body, name="factor", out_shape=jax.ShapeDtypeStruct((n, n), jnp.float32),
        scratch_shapes=[pltpu.VMEM((n, n), jnp.float32), pltpu.VMEM((T, T), jnp.float32),
                        pltpu.VMEM((T, T), jnp.float32)],
        compiler_params=pltpu.CompilerParams(vmem_limit_bytes=32 << 20),
    )(*pieces)


def swap(x, axis, bit):
    return lax.ppermute(x, axis, [(i, i ^ bit) for i in range(lax.axis_size(axis))])


def bits_from(first, count):
    bits = []
    while first < count:
        bits.append(first)
        first *= 2
    return bits


def half_of(x, which, dim):
    size = x.shape[dim] // 2
    return lax.dynamic_slice_in_dim(x, which * size, size, dim)


def reduce_and_factor(mine, send, spectra_total):
    waves, specs = lax.axis_size("wave"), lax.axis_size("spec")
    y = lax.axis_index("spec") % 2
    k = mine.shape[1]
    slots = -(-((k // T) * (k // T + 1) // 2) // (waves // 2))
    other = swap(send, "wave", 1)
    for bit in bits_from(2, waves):
        mine = mine + other
        other = swap(mine, "wave", bit)
    keep, send = gram_blocks(mine, other, slots, 1.0 / spectra_total)
    got = swap(send, "wave", 1)
    mine = half_of(keep, y, 1) + half_of(got, y, 1)
    other = half_of(keep, 1 - y, 1) + half_of(got, 1 - y, 1)
    mine = mine + swap(other, "spec", 1)
    for bit in bits_from(2, specs):
        mine = mine + swap(mine, "spec", bit)
    pieces, offsets = [mine], [(0, 0)]
    steps = [("spec", 1)] + [("wave", b) for b in bits_from(2, waves)] + [("wave", 1)]
    for axis, bit in steps:
        pieces = pieces + [swap(p, axis, bit) for p in pieces]
        offsets = offsets + [(w ^ (bit if axis == "wave" else 0), y_ ^ (bit if axis == "spec" else 0)) for w, y_ in offsets]
    return factor(pieces, offsets, slots, k)


CHUNK = 64


def bell(offset, half_amplitude, inverse_width, wing):
    u = offset * inverse_width
    square = u * u
    value = half_amplitude * (1.0 / (1.0 + square) + jnp.exp2(-square))
    return jnp.where(jnp.abs(offset) <= wing, value, 0.0)


def front(flux, coeffs_t, basis, own, over_core, over_x, wing, strength, widths, sketch_matrix):
    spectra, pixels = flux.shape
    absorbers = own.shape[0] // 3
    half = spectra // 2

    def body(strength_ref, widths_ref, flux_ref, coeffs_ref, basis_ref, own_ref, core_ref, x_ref,
             wing_ref, m_ref, res_ref, keep_ref, send_ref, tau_ref, out_ref):
        w = lax.axis_index("wave")
        core = w % 2
        first = (w * pixels).astype(jnp.float32)
        wing_row = wing_ref[...].astype(jnp.float32)

        def read(ref):
            centre, line, column = (ref[n * absorbers:(n + 1) * absorbers, :] for n in range(3))
            power = jnp.zeros_like(column)
            width = jnp.zeros_like(column)
            for n in range(strength_ref.shape[0]):
                hit = line == float(n)
                power = jnp.where(hit, strength_ref[n], power)
                width = jnp.where(hit, widths_ref[n], width)
            return centre, 0.5 * (column * power), 1.0 / width

        def depth(params, start, count):
            centre, amplitude, inverse = params
            at = lax.broadcasted_iota(jnp.int32, (count, spectra), 0).astype(jnp.float32) + start
            total = None
            for a in range(absorbers):
                one = slice(a, a + 1)
                term = bell(at - centre[one], amplitude[one], inverse[one], wing_row)
                total = term if total is None else total + term
            return total

        mine = read(own_ref)

        def chunk(n, _):
            row = pl.multiple_of(n * CHUNK, CHUNK)
            tau_ref[pl.ds(row, CHUNK), :] = depth(mine, first + row.astype(jnp.float32), CHUNK)
            return 0

        lax.fori_loop(0, pixels // CHUNK, chunk, 0)
        for ref, before in ((core_ref, core == 1), (x_ref, core == 0)):
            row = pl.multiple_of(jnp.where(before, 0, pixels - WING), WING)
            tau_ref[pl.ds(row, WING), :] += depth(read(ref), first + row.astype(jnp.float32), WING)
        for n in range(pixels // T):
            lanes = slice(n * T, (n + 1) * T)
            seen = jnp.exp(-tau_ref[lanes, :].T)
            continuum = lax.dot_general(coeffs_ref[...], basis_ref[:, lanes], (((0,), (0,)), ((), ())),
                                        preferred_element_type=jnp.float32)
            res_ref[:, lanes] = (flux_ref[:, lanes].astype(jnp.float32) - continuum * seen).astype(jnp.bfloat16)
        out_ref[...] = jnp.dot(res_ref[...], m_ref[...], preferred_element_type=jnp.float32)
        keep_ref[...] = out_ref[pl.ds(pl.multiple_of(core * half, half), half), :]
        send_ref[...] = out_ref[pl.ds(pl.multiple_of((1 - core) * half, half), half), :]

    k = sketch_matrix.shape[1]
    smem, vmem = pl.BlockSpec(memory_space=pltpu.SMEM), pl.BlockSpec(memory_space=pltpu.VMEM)
    rows = jax.ShapeDtypeStruct((half, k), jnp.float32)
    return pl.pallas_call(
        body, name="front", in_specs=[smem] * 2 + [vmem] * 8, out_specs=[vmem] * 3,
        out_shape=(jax.ShapeDtypeStruct(flux.shape, jnp.bfloat16), rows, rows),
        scratch_shapes=[pltpu.VMEM((pixels, spectra), jnp.float32), pltpu.VMEM((spectra, k), jnp.float32)],
        compiler_params=pltpu.CompilerParams(vmem_limit_bytes=32 << 20),
    )(strength, widths, flux, coeffs_t, basis, own, over_core, over_x, wing, sketch_matrix)


def shards(
    observed_flux,
    continuum_coeffs,
    continuum_basis,
    centres,
    line_index,
    column_factor,
    wing_width,
    line_strength,
    line_widths,
    sketch_matrix,
):
    waves = lax.axis_size("wave")
    own = jnp.concatenate(
        [centres.T.astype(jnp.float32), line_index.T.astype(jnp.float32), column_factor.T], axis=0)
    across = [(i, (i + 1 if i % 2 else i - 1) % waves) for i in range(waves)]
    over_x = lax.ppermute(own, "wave", across)
    over_core = swap(own, "wave", 1)
    residual, keep, send = front(
        observed_flux, continuum_coeffs.T, continuum_basis, own, over_core, over_x,
        wing_width[None, :], line_strength, line_widths, sketch_matrix)
    return (residual, reduce_and_factor(keep, send, observed_flux.shape[0] * lax.axis_size("spec")))


def solution(mesh):
    return jax.shard_map(
        shards,
        mesh=mesh,
        in_specs=(
            P("spec", "wave"),
            P("spec", None),
            P(None, "wave"),
            P("spec", "wave"),
            P("spec", "wave"),
            P("spec", "wave"),
            P("spec"),
            P(),
            P(),
            P("wave", None),
        ),
        out_specs=(P("spec", "wave"), P()),
        check_vma=False,
    )
```

```python
import jax
import jax.numpy as jnp
from jax import lax
from jax.experimental import pallas as pl
from jax.experimental.pallas import tpu as pltpu
from jax.sharding import PartitionSpec as P

WING = 32
T = 128
S = 8
HI = lax.Precision.HIGHEST

def rows_of(x, k):
    return jnp.broadcast_to(x[k:k + 1, :], x.shape)

def lanes_of(x, c):
    return jnp.broadcast_to(x[:, c:c + 1], x.shape)

def factor_block(d_ref, rk_ref, x_ref):
    steps = T // S
    sub = lax.broadcasted_iota(jnp.int32, (S, T), 0)
    lane = lax.broadcasted_iota(jnp.int32, (S, T), 1)
    at = [sub == k for k in range(S)]
    D = [d_ref[S * g:S * g + S, 0:T] for g in range(steps)]
    E = [jnp.where(lane == sub + S * g, 1.0, 0.0).astype(jnp.float32) for g in range(steps)]
    C = [lanes_of(D[0], k) for k in range(S)]
    for s in range(steps):
        Z = [rows_of(D[s], k) for k in range(S)]
        Y = [rows_of(E[s], k) for k in range(S)]
        B = Cn = None
        if s + 1 < steps:
            B = [lanes_of(D[s + 1], S * s + k) for k in range(S)]
            Cn = [lanes_of(D[s + 1], S * (s + 1) + k) for k in range(S)]
        for k in range(S):
            d = rows_of(C[k], k)
            inv = 1.0 / d
            rs = lax.rsqrt(d)
            rk_ref[S * s + k:S * s + k + 1, :] = (Z[k] * rs)[0:1]
            x_ref[S * s + k:S * s + k + 1, :] = (Y[k] * rs)[0:1]
            Z[k] = Z[k] * inv
            Y[k] = Y[k] * inv
            u = {}
            for c in range(k + 1, S):
                u[c] = rows_of(C[c], k) * inv
                C[c] = jnp.where(at[k], u[c], C[c] - C[k] * u[c])
            for c in range(S):
                if c != k:
                    m = rows_of(C[k], c)
                    Z[c] = Z[c] - m * Z[k]
                    Y[c] = Y[c] - m * Y[k]
            if B is not None:
                bi = B[k] * inv
                for c in range(k + 1, S):
                    B[c] = B[c] - B[k] * u[c]
                for c in range(S):
                    Cn[c] = Cn[c] - bi * rows_of(B[k], c)
        for g in range(s + 1, steps):
            raw = [lanes_of(D[g], S * s + k) for k in range(S)]
            dd, ee = D[g], E[g]
            for k in range(S):
                dd = dd - raw[k] * Z[k]
                ee = ee - raw[k] * Y[k]
            D[g], E[g] = dd, ee
        C = Cn

def upper_block(b, nb):
    i = jnp.int32(0)
    start = jnp.int32(0)
    for r in range(1, nb):
        first = r * nb - r * (r - 1) // 2
        i = i + (b >= first).astype(jnp.int32)
        start = jnp.where(b >= first, first, start)
    return i, i + b - start


def blocks_of(x, slots, t, nb):
    b = jnp.minimum(x * slots + t, nb * (nb + 1) // 2 - 1)
    i, j = upper_block(b, nb)
    return pl.multiple_of(i * T, T), pl.multiple_of(j * T, T)


def gram_blocks(mine, other, slots, scale):
    part, k = mine[0].shape

    def body(*refs):
        mine_refs, other_refs, (keep_ref, send_ref, s_ref, g_ref) = refs[:PARTS], refs[PARTS:2 * PARTS], refs[2 * PARTS:]
        w = lax.axis_index("wave")
        core, x = w % 2, w // 2
        for n in range(PARTS):
            s_ref[n * part:(n + 1) * part, :] = mine_refs[n][...] + other_refs[n][...]
        for t in range(slots):
            i, j = blocks_of(x, slots, t, k // T)
            g_ref[...] = scale * lax.dot_general(
                s_ref[:, pl.ds(i, T)], s_ref[:, pl.ds(j, T)], (((0,), (0,)), ((), ())),
                precision=HI, preferred_element_type=jnp.float32)
            half = T // 2
            keep_ref[t] = g_ref[pl.ds(pl.multiple_of(core * half, half), half), :]
            send_ref[t] = g_ref[pl.ds(pl.multiple_of((1 - core) * half, half), half), :]

    shape = jax.ShapeDtypeStruct((slots, T // 2, T), jnp.float32)
    return pl.pallas_call(
        body, name="gram", out_shape=(shape, shape),
        scratch_shapes=[pltpu.VMEM((PARTS * part, k), jnp.float32), pltpu.VMEM((T, T), jnp.float32)],
        compiler_params=pltpu.CompilerParams(vmem_limit_bytes=32 << 20),
    )(*mine, *other)


def factor(pieces, offsets, slots, n):
    nb = n // T
    part = T // 4

    def body(*refs):
        piece_refs, (r_ref, w_ref, rk_ref, x_ref) = refs[:len(pieces)], refs[len(pieces):]
        w = lax.axis_index("wave")
        y = lax.axis_index("spec") % 2
        for ref, (dw, dy) in zip(piece_refs, offsets):
            v = w ^ dw
            core, x = v % 2, v // 2
            row = pl.multiple_of(core * (T // 2) + (y ^ dy) * part, part)
            for t in range(slots):
                i, j = blocks_of(x, slots, t, nb)
                w_ref[pl.ds(pl.multiple_of(i + row, part), part), pl.ds(j, T)] = ref[t]
        r_ref[...] = jnp.zeros_like(r_ref)
        row = lax.broadcasted_iota(jnp.int32, (T, T), 0)
        col = lax.broadcasted_iota(jnp.int32, (T, T), 1)

        def step(b, _):
            factor_block(w_ref, rk_ref, x_ref)
            base = pl.multiple_of(b * T, T)
            r_ref[pl.ds(base, T), pl.ds(base, T)] = jnp.where(row <= col, rk_ref[...], 0.0)

            @pl.when(b < nb - 1)
            def _():
                x = jnp.where(row >= col, x_ref[...], 0.0)
                panel = jnp.dot(x, w_ref[0:T, T:n], precision=HI, preferred_element_type=jnp.float32)
                for t in range(nb - 1):
                    @pl.when(b + 1 + t < nb)
                    def _():
                        at = pl.multiple_of(base + (t + 1) * T, T)
                        r_ref[pl.ds(base, T), pl.ds(at, T)] = panel[:, t * T:(t + 1) * T]
                for i in range(nb - 1):
                    update = lax.dot_general(
                        panel[:, i * T:(i + 1) * T], panel[:, i * T:], (((0,), (0,)), ((), ())),
                        precision=HI, preferred_element_type=jnp.float32)
                    w_ref[i * T:(i + 1) * T, i * T:n - T] = w_ref[(i + 1) * T:(i + 2) * T, (i + 1) * T:n] - update
            return 0

        lax.fori_loop(0, nb, step, 0)

    return pl.pallas_call(
        body, name="factor", out_shape=jax.ShapeDtypeStruct((n, n), jnp.float32),
        scratch_shapes=[pltpu.VMEM((n, n), jnp.float32), pltpu.VMEM((T, T), jnp.float32),
                        pltpu.VMEM((T, T), jnp.float32)],
        compiler_params=pltpu.CompilerParams(vmem_limit_bytes=32 << 20),
    )(*pieces)


def swap(x, axis, bit):
    return lax.ppermute(x, axis, [(i, i ^ bit) for i in range(lax.axis_size(axis))])


def bits_from(first, count):
    bits = []
    while first < count:
        bits.append(first)
        first *= 2
    return bits


def half_of(x, which, dim):
    size = x.shape[dim] // 2
    return lax.dynamic_slice_in_dim(x, which * size, size, dim)


def reduce_and_factor(mine, send, spectra_total):
    waves, specs = lax.axis_size("wave"), lax.axis_size("spec")
    y = lax.axis_index("spec") % 2
    k = mine[0].shape[1]
    slots = -(-((k // T) * (k // T + 1) // 2) // (waves // 2))
    other = [swap(p, "wave", 1) for p in send]
    for bit in bits_from(2, waves):
        mine = [p + q for p, q in zip(mine, other)]
        other = [swap(p, "wave", bit) for p in mine]
    keep, send = gram_blocks(mine, other, slots, 1.0 / spectra_total)
    got = swap(send, "wave", 1)
    mine = half_of(keep, y, 1) + half_of(got, y, 1)
    other = half_of(keep, 1 - y, 1) + half_of(got, 1 - y, 1)
    mine = mine + swap(other, "spec", 1)
    for bit in bits_from(2, specs):
        mine = mine + swap(mine, "spec", bit)
    pieces, offsets = [mine], [(0, 0)]
    steps = [("spec", 1)] + [("wave", b) for b in bits_from(2, waves)] + [("wave", 1)]
    for axis, bit in steps:
        pieces = pieces + [swap(p, axis, bit) for p in pieces]
        offsets = offsets + [(w ^ (bit if axis == "wave" else 0), y_ ^ (bit if axis == "spec" else 0)) for w, y_ in offsets]
    return factor(pieces, offsets, slots, k)


CHUNK = 64


def bell(offset, half_amplitude, inverse_width, wing):
    u = offset * inverse_width
    square = u * u
    value = half_amplitude * (1.0 / (1.0 + square) + jnp.exp2(-square))
    return jnp.where(jnp.abs(offset) <= wing, value, 0.0)


PARTS = 2
SMEM = pl.BlockSpec(memory_space=pltpu.SMEM)
VMEM = pl.BlockSpec(memory_space=pltpu.VMEM)
HBM = pl.BlockSpec(memory_space=pltpu.HBM)


def line_table(centres, line_index, column_factor, wing, strength, widths):
    absorbers, spectra = centres.shape

    def body(centre_ref, line_ref, column_ref, wing_ref, strength_ref, widths_ref, out_ref,
             c_ref, l_ref, f_ref, g_ref, power_ref, width_ref, sems):
        copies = [pltpu.make_async_copy(source, target, sems.at[n]) for n, (source, target) in enumerate(
            ((strength_ref, power_ref), (widths_ref, width_ref), (line_ref, l_ref), (column_ref, f_ref),
             (centre_ref, c_ref), (wing_ref, g_ref)))]
        for copy in copies:
            copy.start()
        for copy in copies:
            copy.wait()
        line = l_ref[...]
        power = jnp.zeros(line.shape, jnp.float32)
        width = jnp.ones(line.shape, jnp.float32)
        for n in range(strength.shape[0]):
            hit = line == n
            power = jnp.where(hit, power_ref[n], power)
            width = jnp.where(hit, width_ref[n], width)
        out_ref[0:absorbers, :] = c_ref[...].astype(jnp.float32)
        out_ref[absorbers:2 * absorbers, :] = 0.5 * (f_ref[...] * power)
        out_ref[2 * absorbers:3 * absorbers, :] = 1.0 / width
        out_ref[3 * absorbers:4 * absorbers, :] = jnp.broadcast_to(
            g_ref[...].astype(jnp.float32), (absorbers, spectra))

    return pl.pallas_call(
        body, name="lines", in_specs=[HBM] * 6, out_specs=VMEM,
        out_shape=jax.ShapeDtypeStruct((4 * absorbers, spectra), jnp.float32),
        scratch_shapes=[pltpu.VMEM(centres.shape, jnp.int32), pltpu.VMEM(centres.shape, jnp.int32),
                        pltpu.VMEM(centres.shape, jnp.float32), pltpu.VMEM(wing.shape, jnp.int32),
                        pltpu.SMEM(strength.shape, jnp.float32), pltpu.SMEM(widths.shape, jnp.float32),
                        pltpu.SemaphoreType.DMA((6,))],
    )(centres, line_index, column_factor, wing, strength, widths)


def front(flux, coeffs_t, basis, own, over_core, over_x, sketch_matrix):
    spectra, pixels = flux.shape
    absorbers = own.shape[0] // 4
    part = spectra // (2 * PARTS)
    k = sketch_matrix.shape[1]

    def body(flux_hbm, coeffs_hbm, basis_hbm, m_hbm, own_ref, core_ref, x_ref, res_hbm, *refs):
        outs, (flux_ref, coeffs_ref, basis_ref, m_ref, res_ref, tau_ref, sems) = refs[:2 * PARTS], refs[2 * PARTS:]
        loads = [pltpu.make_async_copy(source, target, sems.at[n]) for n, (source, target) in enumerate(
            ((flux_hbm, flux_ref), (coeffs_hbm, coeffs_ref), (basis_hbm, basis_ref), (m_hbm, m_ref)))]
        for copy in loads:
            copy.start()
        w = lax.axis_index("wave")
        core = w % 2
        first = (w * pixels).astype(jnp.float32)
        wing_row = own_ref[3 * absorbers:3 * absorbers + 1, :]

        def depth(ref, start, count):
            at = lax.broadcasted_iota(jnp.int32, (count, spectra), 0).astype(jnp.float32) + start
            total = None
            for a in range(absorbers):
                centre, amplitude, inverse = (ref[n * absorbers + a:n * absorbers + a + 1, :] for n in range(3))
                term = bell(at - centre, amplitude, inverse, wing_row)
                total = term if total is None else total + term
            return total

        def chunk(n, _):
            row = pl.multiple_of(n * CHUNK, CHUNK)
            tau_ref[pl.ds(row, CHUNK), :] = depth(own_ref, first + row.astype(jnp.float32), CHUNK)
            return 0

        lax.fori_loop(0, pixels // CHUNK, chunk, 0)
        for ref, before in ((core_ref, core == 1), (x_ref, core == 0)):
            row = pl.multiple_of(jnp.where(before, 0, pixels - WING), WING)
            tau_ref[pl.ds(row, WING), :] += depth(ref, first + row.astype(jnp.float32), WING)
        for copy in loads[:3]:
            copy.wait()
        for n in range(pixels // T):
            lanes = slice(n * T, (n + 1) * T)
            seen = jnp.exp(-tau_ref[lanes, :].T)
            continuum = lax.dot_general(coeffs_ref[...], basis_ref[:, lanes], (((0,), (0,)), ((), ())),
                                        preferred_element_type=jnp.float32)
            res_ref[:, lanes] = (flux_ref[:, lanes].astype(jnp.float32) - continuum * seen).astype(jnp.bfloat16)
        store = pltpu.make_async_copy(res_ref, res_hbm, sems.at[4])
        store.start()
        loads[3].wait()
        for n, out in enumerate(outs):
            side = core if n < PARTS else 1 - core
            row = pl.multiple_of(side * (spectra // 2) + (n % PARTS) * part, part)
            out[...] = jnp.dot(res_ref[pl.ds(row, part), :], m_ref[...], preferred_element_type=jnp.float32)
        store.wait()

    rows = jax.ShapeDtypeStruct((part, k), jnp.float32)
    outs = pl.pallas_call(
        body, name="front", in_specs=[HBM] * 4 + [VMEM] * 3, out_specs=[HBM] + [VMEM] * (2 * PARTS),
        out_shape=[jax.ShapeDtypeStruct(flux.shape, jnp.bfloat16)] + [rows] * (2 * PARTS),
        scratch_shapes=[pltpu.VMEM(a.shape, a.dtype) for a in (flux, coeffs_t, basis, sketch_matrix, flux)]
        + [pltpu.VMEM((pixels, spectra), jnp.float32), pltpu.SemaphoreType.DMA((5,))],
        compiler_params=pltpu.CompilerParams(vmem_limit_bytes=107 << 19),
    )(flux, coeffs_t, basis, sketch_matrix, own, over_core, over_x)
    return outs[0], outs[1:1 + PARTS], outs[1 + PARTS:]


def shards(
    observed_flux,
    continuum_coeffs,
    continuum_basis,
    centres,
    line_index,
    column_factor,
    wing_width,
    line_strength,
    line_widths,
    sketch_matrix,
):
    waves = lax.axis_size("wave")
    own = line_table(centres.T, line_index.T, column_factor.T, wing_width[None, :], line_strength, line_widths)
    across = [(i, (i + 1 if i % 2 else i - 1) % waves) for i in range(waves)]
    over_x = lax.ppermute(own, "wave", across)
    over_core = swap(own, "wave", 1)
    residual, keep, send = front(
        observed_flux, continuum_coeffs.T, continuum_basis, own, over_core, over_x, sketch_matrix)
    return (residual, reduce_and_factor(keep, send, observed_flux.shape[0] * lax.axis_size("spec")))


def solution(mesh):
    return jax.shard_map(
        shards,
        mesh=mesh,
        in_specs=(
            P("spec", "wave"),
            P("spec", None),
            P(None, "wave"),
            P("spec", "wave"),
            P("spec", "wave"),
            P("spec", "wave"),
            P("spec"),
            P(),
            P(),
            P("wave", None),
        ),
        out_specs=(P("spec", "wave"), P()),
        check_vma=False,
    )
```

```python
import jax
import jax.numpy as jnp
from jax import lax
from jax.experimental import pallas as pl
from jax.experimental.pallas import tpu as pltpu
from jax.sharding import PartitionSpec as P

WING = 32
T = 128
S = 8
HI = lax.Precision.HIGHEST

def rows_of(x, k):
    return jnp.broadcast_to(x[k:k + 1, :], x.shape)

def lanes_of(x, c):
    return jnp.broadcast_to(x[:, c:c + 1], x.shape)

NEAR = 2

def split3(x):
    a = x.astype(jnp.bfloat16)
    r = x - a.astype(jnp.float32)
    b = r.astype(jnp.bfloat16)
    return a, b, (r - b.astype(jnp.float32)).astype(jnp.bfloat16)

def outer(x, y):
    x1, x2, x3 = split3(x)
    y1, y2, y3 = split3(y)
    left = jnp.concatenate([x1, x1, x2, x1, x2, x3], axis=0)
    right = jnp.concatenate([y1, y2, y1, y3, y2, y1], axis=0)
    return lax.dot_general(left, right, (((0,), (0,)), ((), ())), preferred_element_type=jnp.float32)

def factor_block(d_ref, x_ref):
    steps = T // S
    sub = lax.broadcasted_iota(jnp.int32, (S, T), 0)
    lane = lax.broadcasted_iota(jnp.int32, (S, T), 1)
    at = [sub == k for k in range(S)]
    D = [d_ref[S * g:S * g + S, 0:T] for g in range(steps)]
    C = [lanes_of(D[0], k) for k in range(S)]
    later = None
    for s in range(steps):
        done = (lane >= S * s) & (lane < S * s + S)
        rows = D[s]
        start = jnp.where(done, jnp.where(lane == sub + S * s, 1.0, 0.0), rows)
        W = [rows_of(start, k) for k in range(S)]
        B = Cn = None
        if s + 1 < steps:
            B = [lanes_of(D[s + 1], S * s + k) for k in range(S)]
            first = list(B)
            Ca = [None] * S
            Cn = [lanes_of(D[s + 1], S * (s + 1) + k) for k in range(S)]
        for k in range(S):
            d = rows_of(C[k], k)
            inv = 1.0 / d
            x_ref[S * s + k:S * s + k + 1, :] = (W[k] * lax.rsqrt(d))[0:1]
            u = {}
            for c in range(k + 1, S):
                u[c] = rows_of(C[c], k) * inv
                C[c] = jnp.where(at[k], u[c], C[c] - C[k] * u[c])
                W[c] = W[c] - u[c] * W[k]
            W[k] = W[k] * inv
            for c in range(k):
                W[c] = W[c] - rows_of(C[k], c) * W[k]
            if B is not None:
                bi = B[k] * inv
                for c in range(k + 1, S):
                    B[c] = B[c] - B[k] * u[c]
                for c in range(S):
                    v = bi * rows_of(B[k], c)
                    Ca[c] = v if k == 0 else Ca[c] + v
        if later is not None:
            for g, part in later:
                D[g] = D[g] - part
        for g in range(s + 1, min(s + 1 + NEAR, steps)):
            raw = first if g == s + 1 else [lanes_of(D[g], S * s + k) for k in range(S)]
            terms = [raw[k] * W[k] for k in range(S)]
            while len(terms) > 1:
                terms = [p + q for p, q in zip(terms[::2], terms[1::2])]
            D[g] = jnp.where(done, 0.0, D[g]) - terms[0]
        later = None
        if s + 1 + NEAR < steps:
            w = W[S - 1]
            for k in range(S - 1):
                w = jnp.where(at[k], W[k], w)
            full = outer(rows, w)
            later = []
            for g in range(s + 1 + NEAR, steps):
                D[g] = jnp.where(done, 0.0, D[g])
                later.append((g, full[S * g:S * g + S, :]))
        C = [p - q for p, q in zip(Cn, Ca)] if Cn is not None else None

def upper_block(b, nb):
    i = jnp.int32(0)
    start = jnp.int32(0)
    for r in range(1, nb):
        first = r * nb - r * (r - 1) // 2
        i = i + (b >= first).astype(jnp.int32)
        start = jnp.where(b >= first, first, start)
    return i, i + b - start


def blocks_of(x, slots, t, nb):
    b = jnp.minimum(x * slots + t, nb * (nb + 1) // 2 - 1)
    i, j = upper_block(b, nb)
    return pl.multiple_of(i * T, T), pl.multiple_of(j * T, T)


def gram_blocks(mine, other, slots, scale):
    part, k = mine[0].shape

    def body(*refs):
        mine_refs, other_refs, (keep_ref, send_ref, s_ref, g_ref) = refs[:PARTS], refs[PARTS:2 * PARTS], refs[2 * PARTS:]
        w = lax.axis_index("wave")
        core, x = w % 2, w // 2
        for n in range(PARTS):
            s_ref[n * part:(n + 1) * part, :] = mine_refs[n][...] + other_refs[n][...]
        for t in range(slots):
            i, j = blocks_of(x, slots, t, k // T)
            g_ref[...] = scale * lax.dot_general(
                s_ref[:, pl.ds(i, T)], s_ref[:, pl.ds(j, T)], (((0,), (0,)), ((), ())),
                precision=HI, preferred_element_type=jnp.float32)
            half = T // 2
            keep_ref[t] = g_ref[pl.ds(pl.multiple_of(core * half, half), half), :]
            send_ref[t] = g_ref[pl.ds(pl.multiple_of((1 - core) * half, half), half), :]

    shape = jax.ShapeDtypeStruct((slots, T // 2, T), jnp.float32)
    return pl.pallas_call(
        body, name="gram", out_shape=(shape, shape),
        scratch_shapes=[pltpu.VMEM((PARTS * part, k), jnp.float32), pltpu.VMEM((T, T), jnp.float32)],
        compiler_params=pltpu.CompilerParams(vmem_limit_bytes=32 << 20),
    )(*mine, *other)


def factor(pieces, offsets, slots, n):
    nb = n // T
    part = T // 4

    def body(*refs):
        piece_refs, (r_ref, w_ref, x_ref) = refs[:len(pieces)], refs[len(pieces):]
        w = lax.axis_index("wave")
        y = lax.axis_index("spec") % 2
        for ref, (dw, dy) in zip(piece_refs, offsets):
            v = w ^ dw
            core, x = v % 2, v // 2
            row = pl.multiple_of(core * (T // 2) + (y ^ dy) * part, part)
            for t in range(slots):
                i, j = blocks_of(x, slots, t, nb)
                w_ref[pl.ds(pl.multiple_of(i + row, part), part), pl.ds(j, T)] = ref[t]
        r_ref[...] = jnp.zeros_like(r_ref)
        row = lax.broadcasted_iota(jnp.int32, (T, T), 0)
        col = lax.broadcasted_iota(jnp.int32, (T, T), 1)

        def step(b, _):
            factor_block(w_ref, x_ref)
            base = pl.multiple_of(b * T, T)
            x = jnp.where(row >= col, x_ref[...], 0.0)
            diagonal = jnp.dot(x, w_ref[0:T, 0:T], precision=HI, preferred_element_type=jnp.float32)
            r_ref[pl.ds(base, T), pl.ds(base, T)] = jnp.where(row <= col, diagonal, 0.0)

            @pl.when(b < nb - 1)
            def _():
                panel = jnp.dot(x, w_ref[0:T, T:n], precision=HI, preferred_element_type=jnp.float32)
                for t in range(nb - 1):
                    @pl.when(b + 1 + t < nb)
                    def _():
                        at = pl.multiple_of(base + (t + 1) * T, T)
                        r_ref[pl.ds(base, T), pl.ds(at, T)] = panel[:, t * T:(t + 1) * T]
                for i in range(nb - 1):
                    update = lax.dot_general(
                        panel[:, i * T:(i + 1) * T], panel[:, i * T:], (((0,), (0,)), ((), ())),
                        precision=HI, preferred_element_type=jnp.float32)
                    w_ref[i * T:(i + 1) * T, i * T:n - T] = w_ref[(i + 1) * T:(i + 2) * T, (i + 1) * T:n] - update
            return 0

        lax.fori_loop(0, nb, step, 0)

    return pl.pallas_call(
        body, name="factor", out_shape=jax.ShapeDtypeStruct((n, n), jnp.float32),
        scratch_shapes=[pltpu.VMEM((n, n), jnp.float32), pltpu.VMEM((T, T), jnp.float32)],
        compiler_params=pltpu.CompilerParams(vmem_limit_bytes=32 << 20),
    )(*pieces)


def swap(x, axis, bit):
    return lax.ppermute(x, axis, [(i, i ^ bit) for i in range(lax.axis_size(axis))])


def bits_from(first, count):
    bits = []
    while first < count:
        bits.append(first)
        first *= 2
    return bits


def half_of(x, which, dim):
    size = x.shape[dim] // 2
    return lax.dynamic_slice_in_dim(x, which * size, size, dim)


def reduce_and_factor(mine, send, spectra_total):
    waves, specs = lax.axis_size("wave"), lax.axis_size("spec")
    y = lax.axis_index("spec") % 2
    k = mine[0].shape[1]
    slots = -(-((k // T) * (k // T + 1) // 2) // (waves // 2))
    other = [swap(p, "wave", 1) for p in send]
    for bit in bits_from(2, waves):
        mine = [p + q for p, q in zip(mine, other)]
        other = [swap(p, "wave", bit) for p in mine]
    keep, send = gram_blocks(mine, other, slots, 1.0 / spectra_total)
    got = swap(send, "wave", 1)
    mine = half_of(keep, y, 1) + half_of(got, y, 1)
    other = half_of(keep, 1 - y, 1) + half_of(got, 1 - y, 1)
    mine = mine + swap(other, "spec", 1)
    for bit in bits_from(2, specs):
        mine = mine + swap(mine, "spec", bit)
    pieces, offsets = [mine], [(0, 0)]
    steps = [("spec", 1)] + [("wave", b) for b in bits_from(2, waves)] + [("wave", 1)]
    for axis, bit in steps:
        pieces = pieces + [swap(p, axis, bit) for p in pieces]
        offsets = offsets + [(w ^ (bit if axis == "wave" else 0), y_ ^ (bit if axis == "spec" else 0)) for w, y_ in offsets]
    return factor(pieces, offsets, slots, k)


CHUNK = 64


def bell(offset, half_amplitude, inverse_width, wing):
    u = offset * inverse_width
    square = u * u
    value = half_amplitude * (1.0 / (1.0 + square) + jnp.exp2(-square))
    return jnp.where(jnp.abs(offset) <= wing, value, 0.0)


PARTS = 2
SMEM = pl.BlockSpec(memory_space=pltpu.SMEM)
VMEM = pl.BlockSpec(memory_space=pltpu.VMEM)
HBM = pl.BlockSpec(memory_space=pltpu.HBM)


def line_table(centres, line_index, column_factor, wing, strength, widths):
    absorbers, spectra = centres.shape

    def body(centre_ref, line_ref, column_ref, wing_ref, strength_ref, widths_ref, out_ref,
             c_ref, l_ref, f_ref, g_ref, power_ref, width_ref, sems):
        copies = [pltpu.make_async_copy(source, target, sems.at[n]) for n, (source, target) in enumerate(
            ((strength_ref, power_ref), (widths_ref, width_ref), (line_ref, l_ref), (column_ref, f_ref),
             (centre_ref, c_ref), (wing_ref, g_ref)))]
        for copy in copies:
            copy.start()
        for copy in copies:
            copy.wait()
        line = l_ref[...]
        power = jnp.zeros(line.shape, jnp.float32)
        width = jnp.ones(line.shape, jnp.float32)
        for n in range(strength.shape[0]):
            hit = line == n
            power = jnp.where(hit, power_ref[n], power)
            width = jnp.where(hit, width_ref[n], width)
        out_ref[0:absorbers, :] = c_ref[...].astype(jnp.float32)
        out_ref[absorbers:2 * absorbers, :] = 0.5 * (f_ref[...] * power)
        out_ref[2 * absorbers:3 * absorbers, :] = 1.0 / width
        out_ref[3 * absorbers:4 * absorbers, :] = jnp.broadcast_to(
            g_ref[...].astype(jnp.float32), (absorbers, spectra))

    return pl.pallas_call(
        body, name="lines", in_specs=[HBM] * 6, out_specs=VMEM,
        out_shape=jax.ShapeDtypeStruct((4 * absorbers, spectra), jnp.float32),
        scratch_shapes=[pltpu.VMEM(centres.shape, jnp.int32), pltpu.VMEM(centres.shape, jnp.int32),
                        pltpu.VMEM(centres.shape, jnp.float32), pltpu.VMEM(wing.shape, jnp.int32),
                        pltpu.SMEM(strength.shape, jnp.float32), pltpu.SMEM(widths.shape, jnp.float32),
                        pltpu.SemaphoreType.DMA((6,))],
    )(centres, line_index, column_factor, wing, strength, widths)


def front(flux, coeffs_t, basis, own, over_core, over_x, sketch_matrix):
    spectra, pixels = flux.shape
    absorbers = own.shape[0] // 4
    part = spectra // (2 * PARTS)
    k = sketch_matrix.shape[1]

    def body(flux_hbm, coeffs_hbm, basis_hbm, m_hbm, own_ref, core_ref, x_ref, res_hbm, *refs):
        outs, (flux_ref, coeffs_ref, basis_ref, m_ref, res_ref, tau_ref, sems) = refs[:2 * PARTS], refs[2 * PARTS:]
        loads = [pltpu.make_async_copy(source, target, sems.at[n]) for n, (source, target) in enumerate(
            ((flux_hbm, flux_ref), (coeffs_hbm, coeffs_ref), (basis_hbm, basis_ref), (m_hbm, m_ref)))]
        for copy in loads:
            copy.start()
        w = lax.axis_index("wave")
        core = w % 2
        first = (w * pixels).astype(jnp.float32)
        wing_row = own_ref[3 * absorbers:3 * absorbers + 1, :]

        def depth(ref, start, count):
            at = lax.broadcasted_iota(jnp.int32, (count, spectra), 0).astype(jnp.float32) + start
            total = None
            for a in range(absorbers):
                centre, amplitude, inverse = (ref[n * absorbers + a:n * absorbers + a + 1, :] for n in range(3))
                term = bell(at - centre, amplitude, inverse, wing_row)
                total = term if total is None else total + term
            return total

        def chunk(n, _):
            row = pl.multiple_of(n * CHUNK, CHUNK)
            tau_ref[pl.ds(row, CHUNK), :] = depth(own_ref, first + row.astype(jnp.float32), CHUNK)
            return 0

        lax.fori_loop(0, pixels // CHUNK, chunk, 0)
        for ref, before in ((core_ref, core == 1), (x_ref, core == 0)):
            row = pl.multiple_of(jnp.where(before, 0, pixels - WING), WING)
            tau_ref[pl.ds(row, WING), :] += depth(ref, first + row.astype(jnp.float32), WING)
        for copy in loads[:3]:
            copy.wait()
        for n in range(pixels // T):
            lanes = slice(n * T, (n + 1) * T)
            seen = jnp.exp(-tau_ref[lanes, :].T)
            continuum = lax.dot_general(coeffs_ref[...], basis_ref[:, lanes], (((0,), (0,)), ((), ())),
                                        preferred_element_type=jnp.float32)
            res_ref[:, lanes] = (flux_ref[:, lanes].astype(jnp.float32) - continuum * seen).astype(jnp.bfloat16)
        store = pltpu.make_async_copy(res_ref, res_hbm, sems.at[4])
        store.start()
        loads[3].wait()
        for n, out in enumerate(outs):
            side = core if n < PARTS else 1 - core
            row = pl.multiple_of(side * (spectra // 2) + (n % PARTS) * part, part)
            out[...] = jnp.dot(res_ref[pl.ds(row, part), :], m_ref[...], preferred_element_type=jnp.float32)
        store.wait()

    rows = jax.ShapeDtypeStruct((part, k), jnp.float32)
    outs = pl.pallas_call(
        body, name="front", in_specs=[HBM] * 4 + [VMEM] * 3, out_specs=[HBM] + [VMEM] * (2 * PARTS),
        out_shape=[jax.ShapeDtypeStruct(flux.shape, jnp.bfloat16)] + [rows] * (2 * PARTS),
        scratch_shapes=[pltpu.VMEM(a.shape, a.dtype) for a in (flux, coeffs_t, basis, sketch_matrix, flux)]
        + [pltpu.VMEM((pixels, spectra), jnp.float32), pltpu.SemaphoreType.DMA((5,))],
        compiler_params=pltpu.CompilerParams(vmem_limit_bytes=107 << 19),
    )(flux, coeffs_t, basis, sketch_matrix, own, over_core, over_x)
    return outs[0], outs[1:1 + PARTS], outs[1 + PARTS:]


def shards(
    observed_flux,
    continuum_coeffs,
    continuum_basis,
    centres,
    line_index,
    column_factor,
    wing_width,
    line_strength,
    line_widths,
    sketch_matrix,
):
    waves = lax.axis_size("wave")
    own = line_table(centres.T, line_index.T, column_factor.T, wing_width[None, :], line_strength, line_widths)
    across = [(i, (i + 1 if i % 2 else i - 1) % waves) for i in range(waves)]
    over_x = lax.ppermute(own, "wave", across)
    over_core = swap(own, "wave", 1)
    residual, keep, send = front(
        observed_flux, continuum_coeffs.T, continuum_basis, own, over_core, over_x, sketch_matrix)
    return (residual, reduce_and_factor(keep, send, observed_flux.shape[0] * lax.axis_size("spec")))


def solution(mesh):
    return jax.shard_map(
        shards,
        mesh=mesh,
        in_specs=(
            P("spec", "wave"),
            P("spec", None),
            P(None, "wave"),
            P("spec", "wave"),
            P("spec", "wave"),
            P("spec", "wave"),
            P("spec"),
            P(),
            P(),
            P("wave", None),
        ),
        out_specs=(P("spec", "wave"), P()),
        check_vma=False,
    )
```

```python
import jax
import jax.numpy as jnp
from jax import lax
from jax.experimental import pallas as pl
from jax.experimental.pallas import tpu as pltpu
from jax.sharding import PartitionSpec as P

WING = 32
T = 128
S = 8
HI = lax.Precision.HIGHEST

def rows_of(x, k):
    return jnp.broadcast_to(x[k:k + 1, :], x.shape)

def lanes_of(x, c):
    return jnp.broadcast_to(x[:, c:c + 1], x.shape)

NEAR = 2

def split3(x):
    a = x.astype(jnp.bfloat16)
    r = x - a.astype(jnp.float32)
    b = r.astype(jnp.bfloat16)
    return a, b, (r - b.astype(jnp.float32)).astype(jnp.bfloat16)

LEFT, RIGHT = (0, 0, 1, 0, 1, 2), (0, 1, 0, 2, 1, 0)

def stack(parts, order, axis):
    return jnp.concatenate([parts[n] for n in order], axis=axis)

def outer(x, y):
    return lax.dot_general(stack(split3(x), LEFT, 0), stack(split3(y), RIGHT, 0), (((0,), (0,)), ((), ())), preferred_element_type=jnp.float32)

def factor_block(d_ref, x_ref):
    steps = T // S
    sub = lax.broadcasted_iota(jnp.int32, (S, T), 0)
    lane = lax.broadcasted_iota(jnp.int32, (S, T), 1)
    at = [sub == k for k in range(S)]
    D = [d_ref[S * g:S * g + S, 0:T] for g in range(steps)]
    C = [lanes_of(D[0], k) for k in range(S)]
    later = None
    for s in range(steps):
        done = (lane >= S * s) & (lane < S * s + S)
        rows = D[s]
        start = jnp.where(done, jnp.where(lane == sub + S * s, 1.0, 0.0), rows)
        W = [rows_of(start, k) for k in range(S)]
        B = Cn = None
        if s + 1 < steps:
            B = [lanes_of(D[s + 1], S * s + k) for k in range(S)]
            first = list(B)
            Ca = [None] * S
            Cn = [lanes_of(D[s + 1], S * (s + 1) + k) for k in range(S)]
        for k in range(S):
            d = rows_of(C[k], k)
            inv = 1.0 / d
            x_ref[S * s + k:S * s + k + 1, :] = (W[k] * lax.rsqrt(d))[0:1]
            u = {}
            for c in range(k + 1, S):
                u[c] = rows_of(C[c], k) * inv
                C[c] = jnp.where(at[k], u[c], C[c] - C[k] * u[c])
                W[c] = W[c] - u[c] * W[k]
            W[k] = W[k] * inv
            for c in range(k):
                W[c] = W[c] - rows_of(C[k], c) * W[k]
            if B is not None:
                bi = B[k] * inv
                for c in range(k + 1, S):
                    B[c] = B[c] - B[k] * u[c]
                for c in range(S):
                    v = bi * rows_of(B[k], c)
                    Ca[c] = v if k == 0 else Ca[c] + v
        if later is not None:
            for g, part in later:
                D[g] = D[g] - part
        for g in range(s + 1, min(s + 1 + NEAR, steps)):
            raw = first if g == s + 1 else [lanes_of(D[g], S * s + k) for k in range(S)]
            terms = [raw[k] * W[k] for k in range(S)]
            while len(terms) > 1:
                terms = [p + q for p, q in zip(terms[::2], terms[1::2])]
            D[g] = jnp.where(done, 0.0, D[g]) - terms[0]
        later = None
        if s + 1 + NEAR < steps:
            w = W[S - 1]
            for k in range(S - 1):
                w = jnp.where(at[k], W[k], w)
            full = outer(rows, w)
            later = []
            for g in range(s + 1 + NEAR, steps):
                D[g] = jnp.where(done, 0.0, D[g])
                later.append((g, full[S * g:S * g + S, :]))
        C = [p - q for p, q in zip(Cn, Ca)] if Cn is not None else None

def upper_block(b, nb):
    i = jnp.int32(0)
    start = jnp.int32(0)
    for r in range(1, nb):
        first = r * nb - r * (r - 1) // 2
        i = i + (b >= first).astype(jnp.int32)
        start = jnp.where(b >= first, first, start)
    return i, i + b - start


def blocks_of(x, slots, t, nb):
    b = jnp.minimum(x * slots + t, nb * (nb + 1) // 2 - 1)
    i, j = upper_block(b, nb)
    return pl.multiple_of(i * T, T), pl.multiple_of(j * T, T)


def gram_blocks(mine, other, slots, scale):
    part, k = mine[0].shape

    def body(*refs):
        mine_refs, other_refs, (keep_ref, send_ref, s_ref, g_ref) = refs[:PARTS], refs[PARTS:2 * PARTS], refs[2 * PARTS:]
        w = lax.axis_index("wave")
        core, x = w % 2, w // 2
        for n in range(PARTS):
            s_ref[n * part:(n + 1) * part, :] = mine_refs[n][...] + other_refs[n][...]
        for t in range(slots):
            i, j = blocks_of(x, slots, t, k // T)
            g_ref[...] = scale * lax.dot_general(
                s_ref[:, pl.ds(i, T)], s_ref[:, pl.ds(j, T)], (((0,), (0,)), ((), ())),
                precision=HI, preferred_element_type=jnp.float32)
            half = T // 2
            keep_ref[t] = g_ref[pl.ds(pl.multiple_of(core * half, half), half), :]
            send_ref[t] = g_ref[pl.ds(pl.multiple_of((1 - core) * half, half), half), :]

    shape = jax.ShapeDtypeStruct((slots, T // 2, T), jnp.float32)
    return pl.pallas_call(
        body, name="gram", out_shape=(shape, shape),
        scratch_shapes=[pltpu.VMEM((PARTS * part, k), jnp.float32), pltpu.VMEM((T, T), jnp.float32)],
        compiler_params=pltpu.CompilerParams(vmem_limit_bytes=32 << 20),
    )(*mine, *other)


def factor(pieces, offsets, slots, n):
    nb = n // T
    part = T // 4

    def body(*refs):
        piece_refs, (r_ref, w_ref, x_ref) = refs[:len(pieces)], refs[len(pieces):]
        w = lax.axis_index("wave")
        y = lax.axis_index("spec") % 2
        for ref, (dw, dy) in zip(piece_refs, offsets):
            v = w ^ dw
            core, x = v % 2, v // 2
            row = pl.multiple_of(core * (T // 2) + (y ^ dy) * part, part)
            for t in range(slots):
                i, j = blocks_of(x, slots, t, nb)
                w_ref[pl.ds(pl.multiple_of(i + row, part), part), pl.ds(j, T)] = ref[t]
        for b in range(1, nb):
            r_ref[b * T:(b + 1) * T, 0:b * T] = jnp.zeros((T, b * T), jnp.float32)
        row = lax.broadcasted_iota(jnp.int32, (T, T), 0)
        col = lax.broadcasted_iota(jnp.int32, (T, T), 1)

        for b in range(nb):
            low, high = b * T, (b + 1) * T
            factor_block(w_ref.at[low:high, low:high], x_ref)
            inverse = jnp.where(row >= col, x_ref[...], 0.0)
            rows = jnp.dot(stack(split3(inverse), LEFT, 1), stack(split3(w_ref[low:high, low:n]), RIGHT, 0),
                           preferred_element_type=jnp.float32)
            r_ref[low:high, low:high] = jnp.where(row <= col, rows[:, 0:T], 0.0)
            if b == nb - 1:
                break
            r_ref[low:high, high:n] = rows[:, T:]
            right = stack(split3(rows[:, T:]), RIGHT, 0)
            for i in range(b + 1, nb):
                left = stack(split3(rows[:, (i - b) * T:(i - b + 1) * T].T), LEFT, 1)
                w_ref[i * T:(i + 1) * T, i * T:n] -= jnp.dot(
                    left, right[:, (i - b - 1) * T:], preferred_element_type=jnp.float32)

    return pl.pallas_call(
        body, name="factor", out_shape=jax.ShapeDtypeStruct((n, n), jnp.float32),
        scratch_shapes=[pltpu.VMEM((n, n), jnp.float32), pltpu.VMEM((T, T), jnp.float32)],
        compiler_params=pltpu.CompilerParams(vmem_limit_bytes=32 << 20),
    )(*pieces)


def swap(x, axis, bit):
    return lax.ppermute(x, axis, [(i, i ^ bit) for i in range(lax.axis_size(axis))])


def bits_from(first, count):
    bits = []
    while first < count:
        bits.append(first)
        first *= 2
    return bits


def half_of(x, which, dim):
    size = x.shape[dim] // 2
    return lax.dynamic_slice_in_dim(x, which * size, size, dim)


def reduce_and_factor(mine, send, spectra_total):
    waves, specs = lax.axis_size("wave"), lax.axis_size("spec")
    y = lax.axis_index("spec") % 2
    k = mine[0].shape[1]
    slots = -(-((k // T) * (k // T + 1) // 2) // (waves // 2))
    other = [swap(p, "wave", 1) for p in send]
    for bit in bits_from(2, waves):
        mine = [p + q for p, q in zip(mine, other)]
        other = [swap(p, "wave", bit) for p in mine]
    keep, send = gram_blocks(mine, other, slots, 1.0 / spectra_total)
    got = swap(send, "wave", 1)
    mine = half_of(keep, y, 1) + half_of(got, y, 1)
    other = half_of(keep, 1 - y, 1) + half_of(got, 1 - y, 1)
    mine = mine + swap(other, "spec", 1)
    for bit in bits_from(2, specs):
        mine = mine + swap(mine, "spec", bit)
    pieces, offsets = [mine], [(0, 0)]
    steps = [("spec", 1)] + [("wave", b) for b in bits_from(2, waves)] + [("wave", 1)]
    for axis, bit in steps:
        pieces = pieces + [swap(p, axis, bit) for p in pieces]
        offsets = offsets + [(w ^ (bit if axis == "wave" else 0), y_ ^ (bit if axis == "spec" else 0)) for w, y_ in offsets]
    return factor(pieces, offsets, slots, k)


CHUNK = 64


def bell(offset, half_amplitude, inverse_width, wing):
    u = offset * inverse_width
    square = u * u
    value = half_amplitude * (1.0 / (1.0 + square) + jnp.exp2(-square))
    return jnp.where(jnp.abs(offset) <= wing, value, 0.0)


PARTS = 2
SMEM = pl.BlockSpec(memory_space=pltpu.SMEM)
VMEM = pl.BlockSpec(memory_space=pltpu.VMEM)
HBM = pl.BlockSpec(memory_space=pltpu.HBM)


def line_table(centres, line_index, column_factor, wing, strength, widths):
    absorbers, spectra = centres.shape

    def body(centre_ref, line_ref, column_ref, wing_ref, strength_ref, widths_ref, out_ref,
             c_ref, l_ref, f_ref, g_ref, power_ref, width_ref, sems):
        copies = [pltpu.make_async_copy(source, target, sems.at[n]) for n, (source, target) in enumerate(
            ((strength_ref, power_ref), (widths_ref, width_ref), (line_ref, l_ref), (column_ref, f_ref),
             (centre_ref, c_ref), (wing_ref, g_ref)))]
        for copy in copies:
            copy.start()
        for copy in copies:
            copy.wait()
        line = l_ref[...]
        power = jnp.zeros(line.shape, jnp.float32)
        width = jnp.ones(line.shape, jnp.float32)
        for n in range(strength.shape[0]):
            hit = line == n
            power = jnp.where(hit, power_ref[n], power)
            width = jnp.where(hit, width_ref[n], width)
        out_ref[0:absorbers, :] = c_ref[...].astype(jnp.float32)
        out_ref[absorbers:2 * absorbers, :] = 0.5 * (f_ref[...] * power)
        out_ref[2 * absorbers:3 * absorbers, :] = 1.0 / width
        out_ref[3 * absorbers:4 * absorbers, :] = jnp.broadcast_to(
            g_ref[...].astype(jnp.float32), (absorbers, spectra))

    return pl.pallas_call(
        body, name="lines", in_specs=[HBM] * 6, out_specs=VMEM,
        out_shape=jax.ShapeDtypeStruct((4 * absorbers, spectra), jnp.float32),
        scratch_shapes=[pltpu.VMEM(centres.shape, jnp.int32), pltpu.VMEM(centres.shape, jnp.int32),
                        pltpu.VMEM(centres.shape, jnp.float32), pltpu.VMEM(wing.shape, jnp.int32),
                        pltpu.SMEM(strength.shape, jnp.float32), pltpu.SMEM(widths.shape, jnp.float32),
                        pltpu.SemaphoreType.DMA((6,))],
    )(centres, line_index, column_factor, wing, strength, widths)


def front(flux, coeffs_t, basis, own, over_core, over_x, sketch_matrix):
    spectra, pixels = flux.shape
    absorbers = own.shape[0] // 4
    part = spectra // (2 * PARTS)
    k = sketch_matrix.shape[1]

    def body(flux_hbm, coeffs_hbm, basis_hbm, m_hbm, own_ref, core_ref, x_ref, res_hbm, *refs):
        outs, (flux_ref, coeffs_ref, basis_ref, m_ref, res_ref, tau_ref, sems) = refs[:2 * PARTS], refs[2 * PARTS:]
        loads = [pltpu.make_async_copy(source, target, sems.at[n]) for n, (source, target) in enumerate(
            ((flux_hbm, flux_ref), (coeffs_hbm, coeffs_ref), (basis_hbm, basis_ref), (m_hbm, m_ref)))]
        for copy in loads:
            copy.start()
        w = lax.axis_index("wave")
        core = w % 2
        first = (w * pixels).astype(jnp.float32)
        wing_row = own_ref[3 * absorbers:3 * absorbers + 1, :]

        def depth(ref, start, count):
            at = lax.broadcasted_iota(jnp.int32, (count, spectra), 0).astype(jnp.float32) + start
            total = None
            for a in range(absorbers):
                centre, amplitude, inverse = (ref[n * absorbers + a:n * absorbers + a + 1, :] for n in range(3))
                term = bell(at - centre, amplitude, inverse, wing_row)
                total = term if total is None else total + term
            return total

        def chunk(n, _):
            row = pl.multiple_of(n * CHUNK, CHUNK)
            tau_ref[pl.ds(row, CHUNK), :] = depth(own_ref, first + row.astype(jnp.float32), CHUNK)
            return 0

        lax.fori_loop(0, pixels // CHUNK, chunk, 0)
        for ref, before in ((core_ref, core == 1), (x_ref, core == 0)):
            row = pl.multiple_of(jnp.where(before, 0, pixels - WING), WING)
            tau_ref[pl.ds(row, WING), :] += depth(ref, first + row.astype(jnp.float32), WING)
        for copy in loads[:3]:
            copy.wait()
        for n in range(pixels // T):
            lanes = slice(n * T, (n + 1) * T)
            seen = jnp.exp(-tau_ref[lanes, :].T)
            continuum = lax.dot_general(coeffs_ref[...], basis_ref[:, lanes], (((0,), (0,)), ((), ())),
                                        preferred_element_type=jnp.float32)
            res_ref[:, lanes] = (flux_ref[:, lanes].astype(jnp.float32) - continuum * seen).astype(jnp.bfloat16)
        store = pltpu.make_async_copy(res_ref, res_hbm, sems.at[4])
        store.start()
        loads[3].wait()
        for n, out in enumerate(outs):
            side = core if n < PARTS else 1 - core
            row = pl.multiple_of(side * (spectra // 2) + (n % PARTS) * part, part)
            out[...] = jnp.dot(res_ref[pl.ds(row, part), :], m_ref[...], preferred_element_type=jnp.float32)
        store.wait()

    rows = jax.ShapeDtypeStruct((part, k), jnp.float32)
    outs = pl.pallas_call(
        body, name="front", in_specs=[HBM] * 4 + [VMEM] * 3, out_specs=[HBM] + [VMEM] * (2 * PARTS),
        out_shape=[jax.ShapeDtypeStruct(flux.shape, jnp.bfloat16)] + [rows] * (2 * PARTS),
        scratch_shapes=[pltpu.VMEM(a.shape, a.dtype) for a in (flux, coeffs_t, basis, sketch_matrix, flux)]
        + [pltpu.VMEM((pixels, spectra), jnp.float32), pltpu.SemaphoreType.DMA((5,))],
        compiler_params=pltpu.CompilerParams(vmem_limit_bytes=107 << 19),
    )(flux, coeffs_t, basis, sketch_matrix, own, over_core, over_x)
    return outs[0], outs[1:1 + PARTS], outs[1 + PARTS:]


def shards(
    observed_flux,
    continuum_coeffs,
    continuum_basis,
    centres,
    line_index,
    column_factor,
    wing_width,
    line_strength,
    line_widths,
    sketch_matrix,
):
    waves = lax.axis_size("wave")
    own = line_table(centres.T, line_index.T, column_factor.T, wing_width[None, :], line_strength, line_widths)
    across = [(i, (i + 1 if i % 2 else i - 1) % waves) for i in range(waves)]
    over_x = lax.ppermute(own, "wave", across)
    over_core = swap(own, "wave", 1)
    residual, keep, send = front(
        observed_flux, continuum_coeffs.T, continuum_basis, jnp.maximum(own, 0.0), over_core, over_x, sketch_matrix)
    return (residual, reduce_and_factor(keep, send, observed_flux.shape[0] * lax.axis_size("spec")))


def solution(mesh):
    return jax.shard_map(
        shards,
        mesh=mesh,
        in_specs=(
            P("spec", "wave"),
            P("spec", None),
            P(None, "wave"),
            P("spec", "wave"),
            P("spec", "wave"),
            P("spec", "wave"),
            P("spec"),
            P(),
            P(),
            P("wave", None),
        ),
        out_specs=(P("spec", "wave"), P()),
        check_vma=False,
    )
```

```python
import jax
import jax.numpy as jnp
from jax import lax
from jax.experimental import pallas as pl
from jax.experimental.pallas import tpu as pltpu
from jax.sharding import PartitionSpec as P

WING = 32
T = 128
S = 8
HI = lax.Precision.HIGHEST

def rows_of(x, k):
    return jnp.broadcast_to(x[k:k + 1, :], x.shape)

def lanes_of(x, c):
    return jnp.broadcast_to(x[:, c:c + 1], x.shape)

NEAR = 2

def split3(x):
    a = x.astype(jnp.bfloat16)
    r = x - a.astype(jnp.float32)
    b = r.astype(jnp.bfloat16)
    return a, b, (r - b.astype(jnp.float32)).astype(jnp.bfloat16)

LEFT, RIGHT = (0, 0, 1, 0, 1, 2), (0, 1, 0, 2, 1, 0)

def stack(parts, order, axis):
    return jnp.concatenate([parts[n] for n in order], axis=axis)

def outer(x, y):
    return lax.dot_general(stack(split3(x), LEFT, 0), stack(split3(y), RIGHT, 0), (((0,), (0,)), ((), ())), preferred_element_type=jnp.float32)

def factor_block(d_ref, x_ref):
    steps = T // S
    sub = lax.broadcasted_iota(jnp.int32, (S, T), 0)
    lane = lax.broadcasted_iota(jnp.int32, (S, T), 1)
    at = [sub == k for k in range(S)]
    D = [d_ref[S * g:S * g + S, 0:T] for g in range(steps)]
    C = [lanes_of(D[0], k) for k in range(S)]
    later = None
    for s in range(steps):
        done = (lane >= S * s) & (lane < S * s + S)
        rows = D[s]
        start = jnp.where(done, jnp.where(lane == sub + S * s, 1.0, 0.0), rows)
        W = [rows_of(start, k) for k in range(S)]
        B = Cn = None
        if s + 1 < steps:
            B = [lanes_of(D[s + 1], S * s + k) for k in range(S)]
            first = list(B)
            Ca = [None] * S
            Cn = [lanes_of(D[s + 1], S * (s + 1) + k) for k in range(S)]
        for k in range(S):
            d = rows_of(C[k], k)
            inv = 1.0 / d
            x_ref[S * s + k:S * s + k + 1, :] = (W[k] * lax.rsqrt(d))[0:1]
            u = {}
            for c in range(k + 1, S):
                u[c] = rows_of(C[c], k) * inv
                C[c] = jnp.where(at[k], u[c], C[c] - C[k] * u[c])
                W[c] = W[c] - u[c] * W[k]
            W[k] = W[k] * inv
            for c in range(k):
                W[c] = W[c] - rows_of(C[k], c) * W[k]
            if B is not None:
                bi = B[k] * inv
                for c in range(k + 1, S):
                    B[c] = B[c] - B[k] * u[c]
                for c in range(S):
                    v = bi * rows_of(B[k], c)
                    Ca[c] = v if k == 0 else Ca[c] + v
        if later is not None:
            for g, part in later:
                D[g] = D[g] - part
        for g in range(s + 1, min(s + 1 + NEAR, steps)):
            raw = first if g == s + 1 else [lanes_of(D[g], S * s + k) for k in range(S)]
            terms = [raw[k] * W[k] for k in range(S)]
            while len(terms) > 1:
                terms = [p + q for p, q in zip(terms[::2], terms[1::2])]
            D[g] = jnp.where(done, 0.0, D[g]) - terms[0]
        later = None
        if s + 1 + NEAR < steps:
            w = W[S - 1]
            for k in range(S - 1):
                w = jnp.where(at[k], W[k], w)
            full = outer(rows, w)
            later = []
            for g in range(s + 1 + NEAR, steps):
                D[g] = jnp.where(done, 0.0, D[g])
                later.append((g, full[S * g:S * g + S, :]))
        C = [p - q for p, q in zip(Cn, Ca)] if Cn is not None else None

def upper_block(b, nb):
    i = jnp.int32(0)
    start = jnp.int32(0)
    for r in range(1, nb):
        first = r * nb - r * (r - 1) // 2
        i = i + (b >= first).astype(jnp.int32)
        start = jnp.where(b >= first, first, start)
    return i, i + b - start


def blocks_of(x, slots, t, nb):
    b = jnp.minimum(x * slots + t, nb * (nb + 1) // 2 - 1)
    i, j = upper_block(b, nb)
    return pl.multiple_of(i * T, T), pl.multiple_of(j * T, T)


def gram_blocks(mine, other, slots, scale):
    part, k = mine[0].shape

    def body(*refs):
        mine_refs, other_refs, (keep_ref, send_ref, s_ref, g_ref) = refs[:PARTS], refs[PARTS:2 * PARTS], refs[2 * PARTS:]
        w = lax.axis_index("wave")
        core, x = w % 2, w // 2
        for n in range(PARTS):
            s_ref[n * part:(n + 1) * part, :] = mine_refs[n][...] + other_refs[n][...]
        for t in range(slots):
            i, j = blocks_of(x, slots, t, k // T)
            g_ref[...] = scale * lax.dot_general(
                s_ref[:, pl.ds(i, T)], s_ref[:, pl.ds(j, T)], (((0,), (0,)), ((), ())),
                precision=HI, preferred_element_type=jnp.float32)
            half = T // 2
            keep_ref[t] = g_ref[pl.ds(pl.multiple_of(core * half, half), half), :]
            send_ref[t] = g_ref[pl.ds(pl.multiple_of((1 - core) * half, half), half), :]

    shape = jax.ShapeDtypeStruct((slots, T // 2, T), jnp.float32)
    return pl.pallas_call(
        body, name="gram", out_shape=(shape, shape),
        scratch_shapes=[pltpu.VMEM((PARTS * part, k), jnp.float32), pltpu.VMEM((T, T), jnp.float32)],
        compiler_params=pltpu.CompilerParams(vmem_limit_bytes=32 << 20),
    )(*mine, *other)


def factor(pieces, offsets, slots, n):
    nb = n // T
    part = T // 4

    def body(*refs):
        piece_refs, (r_ref, w_ref, x_ref) = refs[:len(pieces)], refs[len(pieces):]
        w = lax.axis_index("wave")
        y = lax.axis_index("spec") % 2
        for ref, (dw, dy) in zip(piece_refs, offsets):
            v = w ^ dw
            core, x = v % 2, v // 2
            row = pl.multiple_of(core * (T // 2) + (y ^ dy) * part, part)
            for t in range(slots):
                i, j = blocks_of(x, slots, t, nb)
                w_ref[pl.ds(pl.multiple_of(i + row, part), part), pl.ds(j, T)] = ref[t]
        for b in range(1, nb):
            r_ref[b * T:(b + 1) * T, 0:b * T] = jnp.zeros((T, b * T), jnp.float32)
        row = lax.broadcasted_iota(jnp.int32, (T, T), 0)
        col = lax.broadcasted_iota(jnp.int32, (T, T), 1)

        for b in range(nb):
            low, high = b * T, (b + 1) * T
            factor_block(w_ref.at[low:high, low:high], x_ref)
            inverse = jnp.where(row >= col, x_ref[...], 0.0)
            rows = jnp.dot(stack(split3(inverse), LEFT, 1), stack(split3(w_ref[low:high, low:n]), RIGHT, 0),
                           preferred_element_type=jnp.float32)
            r_ref[low:high, low:high] = jnp.where(row <= col, rows[:, 0:T], 0.0)
            if b == nb - 1:
                break
            r_ref[low:high, high:n] = rows[:, T:]
            right = stack(split3(rows[:, T:]), RIGHT, 0)
            for i in range(b + 1, nb):
                left = stack(split3(rows[:, (i - b) * T:(i - b + 1) * T].T), LEFT, 1)
                w_ref[i * T:(i + 1) * T, i * T:n] -= jnp.dot(
                    left, right[:, (i - b - 1) * T:], preferred_element_type=jnp.float32)

    return pl.pallas_call(
        body, name="factor", out_shape=jax.ShapeDtypeStruct((n, n), jnp.float32),
        scratch_shapes=[pltpu.VMEM((n, n), jnp.float32), pltpu.VMEM((T, T), jnp.float32)],
        compiler_params=pltpu.CompilerParams(vmem_limit_bytes=32 << 20),
    )(*pieces)


def swap(x, axis, bit):
    return lax.ppermute(x, axis, [(i, i ^ bit) for i in range(lax.axis_size(axis))])


def bits_from(first, count):
    bits = []
    while first < count:
        bits.append(first)
        first *= 2
    return bits


def half_of(x, which, dim):
    size = x.shape[dim] // 2
    return lax.dynamic_slice_in_dim(x, which * size, size, dim)


def reduce_and_factor(mine, send, spectra_total):
    waves, specs = lax.axis_size("wave"), lax.axis_size("spec")
    y = lax.axis_index("spec") % 2
    k = mine[0].shape[1]
    slots = -(-((k // T) * (k // T + 1) // 2) // (waves // 2))
    other = [swap(p, "wave", 1) for p in send]
    for bit in bits_from(2, waves):
        mine = [p + q for p, q in zip(mine, other)]
        other = [swap(p, "wave", bit) for p in mine]
    keep, send = gram_blocks(mine, other, slots, 1.0 / spectra_total)
    got = swap(send, "wave", 1)
    mine = half_of(keep, y, 1) + half_of(got, y, 1)
    other = half_of(keep, 1 - y, 1) + half_of(got, 1 - y, 1)
    mine = mine + swap(other, "spec", 1)
    for bit in bits_from(2, specs):
        mine = mine + swap(mine, "spec", bit)
    pieces, offsets = [mine], [(0, 0)]
    steps = [("spec", 1)] + [("wave", b) for b in bits_from(2, waves)] + [("wave", 1)]
    for axis, bit in steps:
        pieces = pieces + [swap(p, axis, bit) for p in pieces]
        offsets = offsets + [(w ^ (bit if axis == "wave" else 0), y_ ^ (bit if axis == "spec" else 0)) for w, y_ in offsets]
    return factor(pieces, offsets, slots, k)


CHUNK = 64


def bell(offset, half_amplitude, inverse_width, wing):
    u = offset * inverse_width
    square = u * u
    value = half_amplitude * (1.0 / (1.0 + square) + jnp.exp2(-square))
    return jnp.where(jnp.abs(offset) <= wing, value, 0.0)


PARTS = 2
FRONT_VMEM = 107 << 19
SMEM = pl.BlockSpec(memory_space=pltpu.SMEM)
VMEM = pl.BlockSpec(memory_space=pltpu.VMEM)
HBM = pl.BlockSpec(memory_space=pltpu.HBM)


def line_table(centres, line_index, column_factor, wing, strength, widths):
    absorbers, spectra = centres.shape

    def body(centre_ref, line_ref, column_ref, wing_ref, strength_ref, widths_ref, out_ref,
             c_ref, l_ref, f_ref, g_ref, power_ref, width_ref, sems):
        copies = [pltpu.make_async_copy(source, target, sems.at[n]) for n, (source, target) in enumerate(
            ((strength_ref, power_ref), (widths_ref, width_ref), (line_ref, l_ref), (column_ref, f_ref),
             (centre_ref, c_ref), (wing_ref, g_ref)))]
        for copy in copies:
            copy.start()
        for copy in copies:
            copy.wait()
        line = l_ref[...]
        power = jnp.zeros(line.shape, jnp.float32)
        width = jnp.ones(line.shape, jnp.float32)
        for n in range(strength.shape[0]):
            hit = line == n
            power = jnp.where(hit, power_ref[n], power)
            width = jnp.where(hit, width_ref[n], width)
        out_ref[0:absorbers, :] = c_ref[...].astype(jnp.float32)
        out_ref[absorbers:2 * absorbers, :] = 0.5 * (f_ref[...] * power)
        out_ref[2 * absorbers:3 * absorbers, :] = 1.0 / width
        out_ref[3 * absorbers:4 * absorbers, :] = jnp.broadcast_to(
            g_ref[...].astype(jnp.float32), (absorbers, spectra))

    return pl.pallas_call(
        body, name="lines", in_specs=[HBM] * 6, out_specs=VMEM,
        out_shape=jax.ShapeDtypeStruct((4 * absorbers, spectra), jnp.float32),
        scratch_shapes=[pltpu.VMEM(centres.shape, jnp.int32), pltpu.VMEM(centres.shape, jnp.int32),
                        pltpu.VMEM(centres.shape, jnp.float32), pltpu.VMEM(wing.shape, jnp.int32),
                        pltpu.SMEM(strength.shape, jnp.float32), pltpu.SMEM(widths.shape, jnp.float32),
                        pltpu.SemaphoreType.DMA((6,))],
    )(centres, line_index, column_factor, wing, strength, widths)


def front(n, flux, coeffs_t, basis, own, over_core, over_x, sketch_matrix, residual):
    spectra, pixels = flux.shape
    count = spectra // PARTS
    absorbers = own.shape[0] // 4
    k = sketch_matrix.shape[1]
    mine = slice(n * count, (n + 1) * count)

    def body(flux_hbm, coeffs_hbm, basis_hbm, m_hbm, own_ref, core_ref, x_ref, *refs):
        res_hbm, keep_ref, send_ref, flux_ref, coeffs_ref, basis_ref, m_ref, res_ref, tau_ref, sems = refs[-10:]
        loads = [pltpu.make_async_copy(source, target, sems.at[i]) for i, (source, target) in enumerate(
            ((flux_hbm.at[mine, :], flux_ref), (coeffs_hbm, coeffs_ref), (basis_hbm, basis_ref), (m_hbm, m_ref)))]
        for copy in loads:
            copy.start()
        w = lax.axis_index("wave")
        core = w % 2
        first = (w * pixels).astype(jnp.float32)
        wing_row = own_ref[3 * absorbers:3 * absorbers + 1, mine]

        def depth(ref, start, height):
            at = lax.broadcasted_iota(jnp.int32, (height, count), 0).astype(jnp.float32) + start
            total = None
            for a in range(absorbers):
                centre, amplitude, inverse = (
                    ref[i * absorbers + a:i * absorbers + a + 1, mine] for i in range(3))
                term = bell(at - centre, amplitude, inverse, wing_row)
                total = term if total is None else total + term
            return total

        def chunk(i, _):
            row = pl.multiple_of(i * CHUNK, CHUNK)
            tau_ref[pl.ds(row, CHUNK), :] = depth(own_ref, first + row.astype(jnp.float32), CHUNK)
            return 0

        lax.fori_loop(0, pixels // CHUNK, chunk, 0)
        for ref, before in ((core_ref, core == 1), (x_ref, core == 0)):
            row = pl.multiple_of(jnp.where(before, 0, pixels - WING), WING)
            tau_ref[pl.ds(row, WING), :] += depth(ref, first + row.astype(jnp.float32), WING)
        for copy in loads[:3]:
            copy.wait()
        for i in range(pixels // T):
            lanes = slice(i * T, (i + 1) * T)
            seen = jnp.exp(-tau_ref[lanes, :].T)
            continuum = lax.dot_general(coeffs_ref[:, mine], basis_ref[:, lanes], (((0,), (0,)), ((), ())),
                                        preferred_element_type=jnp.float32)
            res_ref[:, lanes] = (flux_ref[:, lanes].astype(jnp.float32) - continuum * seen).astype(jnp.bfloat16)
        store = pltpu.make_async_copy(res_ref, res_hbm.at[mine, :], sems.at[4])
        store.start()
        loads[3].wait()
        half = count // 2
        for out, side in ((send_ref, 1 - core), (keep_ref, core)):
            row = pl.multiple_of(side * half, half)
            out[...] = jnp.dot(res_ref[pl.ds(row, half), :], m_ref[...], preferred_element_type=jnp.float32)
        store.wait()

    rows = jax.ShapeDtypeStruct((count // 2, k), jnp.float32)
    earlier = [] if residual is None else [residual]
    return pl.pallas_call(
        body, name="front", in_specs=[HBM] * 4 + [VMEM] * 3 + [HBM] * len(earlier), out_specs=[HBM, VMEM, VMEM],
        out_shape=[jax.ShapeDtypeStruct(flux.shape, jnp.bfloat16), rows, rows],
        input_output_aliases={7: 0} if earlier else {},
        scratch_shapes=[pltpu.VMEM((count, pixels), flux.dtype)]
        + [pltpu.VMEM(a.shape, a.dtype) for a in (coeffs_t, basis, sketch_matrix)]
        + [pltpu.VMEM((count, pixels), jnp.bfloat16), pltpu.VMEM((pixels, count), jnp.float32),
           pltpu.SemaphoreType.DMA((5,))],
        cost_estimate=pl.CostEstimate(flops=2 * count * pixels * k, transcendentals=0,
                                      bytes_accessed=4 * count * pixels + 2 * pixels * k),
        compiler_params=pltpu.CompilerParams(vmem_limit_bytes=FRONT_VMEM),
    )(flux, coeffs_t, basis, sketch_matrix, own, over_core, over_x, *earlier)


def shards(
    observed_flux,
    continuum_coeffs,
    continuum_basis,
    centres,
    line_index,
    column_factor,
    wing_width,
    line_strength,
    line_widths,
    sketch_matrix,
):
    waves = lax.axis_size("wave")
    own = line_table(centres.T, line_index.T, column_factor.T, wing_width[None, :], line_strength, line_widths)
    across = [(i, (i + 1 if i % 2 else i - 1) % waves) for i in range(waves)]
    over_x = lax.ppermute(own, "wave", across)
    over_core = swap(own, "wave", 1)
    here = jnp.maximum(own, 0.0)
    residual, keep, send = None, [], []
    for n in range(PARTS):
        residual, stays, goes = front(n, observed_flux, continuum_coeffs.T, continuum_basis, here,
                                      over_core, over_x, sketch_matrix, residual)
        keep.append(stays)
        send.append(goes)
    return (residual, reduce_and_factor(keep, send, observed_flux.shape[0] * lax.axis_size("spec")))


def solution(mesh):
    return jax.shard_map(
        shards,
        mesh=mesh,
        in_specs=(
            P("spec", "wave"),
            P("spec", None),
            P(None, "wave"),
            P("spec", "wave"),
            P("spec", "wave"),
            P("spec", "wave"),
            P("spec"),
            P(),
            P(),
            P("wave", None),
        ),
        out_specs=(P("spec", "wave"), P()),
        check_vma=False,
    )
```

```python
import jax
import jax.numpy as jnp
from jax import lax
from jax.experimental import pallas as pl
from jax.experimental.pallas import tpu as pltpu
from jax.sharding import PartitionSpec as P

WING = 32
T = 128
S = 8
HI = lax.Precision.HIGHEST

def rows_of(x, k):
    return jnp.broadcast_to(x[k:k + 1, :], x.shape)

def lanes_of(x, c):
    return jnp.broadcast_to(x[:, c:c + 1], x.shape)

NEAR = 2

def split3(x):
    a = x.astype(jnp.bfloat16)
    r = x - a.astype(jnp.float32)
    b = r.astype(jnp.bfloat16)
    return a, b, (r - b.astype(jnp.float32)).astype(jnp.bfloat16)

LEFT, RIGHT = (0, 0, 1, 0, 1, 2), (0, 1, 0, 2, 1, 0)

def stack(parts, order, axis):
    return jnp.concatenate([parts[n] for n in order], axis=axis)

def outer(x, y):
    return lax.dot_general(stack(split3(x), LEFT, 0), stack(split3(y), RIGHT, 0), (((0,), (0,)), ((), ())), preferred_element_type=jnp.float32)

def factor_block(d_ref, x_ref):
    steps = T // S
    sub = lax.broadcasted_iota(jnp.int32, (S, T), 0)
    lane = lax.broadcasted_iota(jnp.int32, (S, T), 1)
    at = [sub == k for k in range(S)]
    D = [d_ref[S * g:S * g + S, 0:T] for g in range(steps)]
    C = [lanes_of(D[0], k) for k in range(S)]
    later = None
    for s in range(steps):
        done = (lane >= S * s) & (lane < S * s + S)
        rows = D[s]
        start = jnp.where(done, jnp.where(lane == sub + S * s, 1.0, 0.0), rows)
        W = [rows_of(start, k) for k in range(S)]
        B = Cn = None
        if s + 1 < steps:
            B = [lanes_of(D[s + 1], S * s + k) for k in range(S)]
            first = list(B)
            Ca = [None] * S
            Cn = [lanes_of(D[s + 1], S * (s + 1) + k) for k in range(S)]
        for k in range(S):
            d = rows_of(C[k], k)
            inv = 1.0 / d
            x_ref[S * s + k:S * s + k + 1, :] = (W[k] * lax.rsqrt(d))[0:1]
            u = {}
            for c in range(k + 1, S):
                u[c] = rows_of(C[c], k) * inv
                C[c] = jnp.where(at[k], u[c], C[c] - C[k] * u[c])
                W[c] = W[c] - u[c] * W[k]
            W[k] = W[k] * inv
            for c in range(k):
                W[c] = W[c] - rows_of(C[k], c) * W[k]
            if B is not None:
                bi = B[k] * inv
                for c in range(k + 1, S):
                    B[c] = B[c] - B[k] * u[c]
                for c in range(S):
                    v = bi * rows_of(B[k], c)
                    Ca[c] = v if k == 0 else Ca[c] + v
        if later is not None:
            for g, part in later:
                D[g] = D[g] - part
        for g in range(s + 1, min(s + 1 + NEAR, steps)):
            raw = first if g == s + 1 else [lanes_of(D[g], S * s + k) for k in range(S)]
            terms = [raw[k] * W[k] for k in range(S)]
            while len(terms) > 1:
                terms = [p + q for p, q in zip(terms[::2], terms[1::2])]
            D[g] = jnp.where(done, 0.0, D[g]) - terms[0]
        later = None
        if s + 1 + NEAR < steps:
            w = W[S - 1]
            for k in range(S - 1):
                w = jnp.where(at[k], W[k], w)
            full = outer(rows, w)
            later = []
            for g in range(s + 1 + NEAR, steps):
                D[g] = jnp.where(done, 0.0, D[g])
                later.append((g, full[S * g:S * g + S, :]))
        C = [p - q for p, q in zip(Cn, Ca)] if Cn is not None else None

def upper_block(b, nb):
    i = jnp.int32(0)
    start = jnp.int32(0)
    for r in range(1, nb):
        first = r * nb - r * (r - 1) // 2
        i = i + (b >= first).astype(jnp.int32)
        start = jnp.where(b >= first, first, start)
    return i, i + b - start


def blocks_of(x, slots, t, nb):
    b = jnp.minimum(x * slots + t, nb * (nb + 1) // 2 - 1)
    i, j = upper_block(b, nb)
    return pl.multiple_of(i * T, T), pl.multiple_of(j * T, T)


def gram_blocks(mine, other, slots, scale):
    part, k = mine[0].shape

    def body(*refs):
        mine_refs, other_refs, (keep_ref, send_ref, s_ref, g_ref) = refs[:PARTS], refs[PARTS:2 * PARTS], refs[2 * PARTS:]
        w = lax.axis_index("wave")
        core, x = w % 2, w // 2
        for n in range(PARTS):
            s_ref[n * part:(n + 1) * part, :] = mine_refs[n][...] + other_refs[n][...]
        for t in range(slots):
            i, j = blocks_of(x, slots, t, k // T)
            g_ref[...] = scale * lax.dot_general(
                s_ref[:, pl.ds(i, T)], s_ref[:, pl.ds(j, T)], (((0,), (0,)), ((), ())),
                precision=HI, preferred_element_type=jnp.float32)
            half = T // 2
            keep_ref[t] = g_ref[pl.ds(pl.multiple_of(core * half, half), half), :]
            send_ref[t] = g_ref[pl.ds(pl.multiple_of((1 - core) * half, half), half), :]

    shape = jax.ShapeDtypeStruct((slots, T // 2, T), jnp.float32)
    return pl.pallas_call(
        body, name="gram", out_shape=(shape, shape),
        scratch_shapes=[pltpu.VMEM((PARTS * part, k), jnp.float32), pltpu.VMEM((T, T), jnp.float32)],
        compiler_params=pltpu.CompilerParams(vmem_limit_bytes=32 << 20),
    )(*mine, *other)


def factor(pieces, offsets, slots, n):
    nb = n // T
    part = T // 4

    def body(*refs):
        piece_refs, (r_ref, w_ref, x_ref) = refs[:len(pieces)], refs[len(pieces):]
        w = lax.axis_index("wave")
        y = lax.axis_index("spec") % 2
        blocks = {}
        for ref, (dw, dy) in zip(piece_refs, offsets):
            if dw // 2 not in blocks:
                blocks[dw // 2] = [blocks_of((w // 2) ^ (dw // 2), slots, t, nb) for t in range(slots)]
            row = ((w % 2) ^ (dw % 2)) * (T // 2) + (y ^ dy) * part
            for t, (i, j) in enumerate(blocks[dw // 2]):
                w_ref[pl.ds(pl.multiple_of(i + row, part), part), pl.ds(j, T)] = ref[t]
        for b in range(1, nb):
            r_ref[b * T:(b + 1) * T, 0:b * T] = jnp.zeros((T, b * T), jnp.float32)
        row = lax.broadcasted_iota(jnp.int32, (T, T), 0)
        col = lax.broadcasted_iota(jnp.int32, (T, T), 1)

        for b in range(nb):
            low, high = b * T, (b + 1) * T
            factor_block(w_ref.at[low:high, low:high], x_ref)
            inverse = jnp.where(row >= col, x_ref[...], 0.0)
            rows = jnp.dot(stack(split3(inverse), LEFT, 1), stack(split3(w_ref[low:high, low:n]), RIGHT, 0),
                           preferred_element_type=jnp.float32)
            r_ref[low:high, low:high] = jnp.where(row <= col, rows[:, 0:T], 0.0)
            if b == nb - 1:
                break
            r_ref[low:high, high:n] = rows[:, T:]
            right = stack(split3(rows[:, T:]), RIGHT, 0)
            for i in range(b + 1, nb):
                left = stack(split3(rows[:, (i - b) * T:(i - b + 1) * T].T), LEFT, 1)
                w_ref[i * T:(i + 1) * T, i * T:n] -= jnp.dot(
                    left, right[:, (i - b - 1) * T:], preferred_element_type=jnp.float32)

    return pl.pallas_call(
        body, name="factor", out_shape=jax.ShapeDtypeStruct((n, n), jnp.float32),
        scratch_shapes=[pltpu.VMEM((n, n), jnp.float32), pltpu.VMEM((T, T), jnp.float32)],
        compiler_params=pltpu.CompilerParams(vmem_limit_bytes=32 << 20),
    )(*pieces)


def swap(x, axis, bit):
    return lax.ppermute(x, axis, [(i, i ^ bit) for i in range(lax.axis_size(axis))])


def bits_from(first, count):
    bits = []
    while first < count:
        bits.append(first)
        first *= 2
    return bits


def half_of(x, which, dim):
    size = x.shape[dim] // 2
    return lax.dynamic_slice_in_dim(x, which * size, size, dim)


def reduce_and_factor(mine, send, spectra_total):
    waves, specs = lax.axis_size("wave"), lax.axis_size("spec")
    y = lax.axis_index("spec") % 2
    k = mine[0].shape[1]
    slots = -(-((k // T) * (k // T + 1) // 2) // (waves // 2))
    other = [swap(p, "wave", 1) for p in send]
    for bit in bits_from(2, waves):
        mine = [p + q for p, q in zip(mine, other)]
        other = [swap(p, "wave", bit) for p in mine]
    keep, send = gram_blocks(mine, other, slots, 1.0 / spectra_total)
    got = swap(send, "wave", 1)
    mine = half_of(keep, y, 1) + half_of(got, y, 1)
    other = half_of(keep, 1 - y, 1) + half_of(got, 1 - y, 1)
    mine = mine + swap(other, "spec", 1)
    for bit in bits_from(2, specs):
        mine = mine + swap(mine, "spec", bit)
    pieces, offsets = [mine], [(0, 0)]
    steps = [("spec", 1)] + [("wave", b) for b in bits_from(2, waves)] + [("wave", 1)]
    for axis, bit in steps:
        pieces = pieces + [swap(p, axis, bit) for p in pieces]
        offsets = offsets + [(w ^ (bit if axis == "wave" else 0), y_ ^ (bit if axis == "spec" else 0)) for w, y_ in offsets]
    return factor(pieces, offsets, slots, k)


CHUNK = 32


def bell(offset, half_amplitude, inverse_width, wing):
    u = offset * inverse_width
    square = u * u
    value = half_amplitude * (1.0 / (1.0 + square) + jnp.exp2(-square))
    return jnp.where(jnp.abs(offset) <= wing, value, 0.0)


PARTS = 2
FRONT_VMEM = 107 << 19
SMEM = pl.BlockSpec(memory_space=pltpu.SMEM)
VMEM = pl.BlockSpec(memory_space=pltpu.VMEM)
HBM = pl.BlockSpec(memory_space=pltpu.HBM)


def line_table(centres, line_index, column_factor, wing, strength, widths):
    absorbers, spectra = centres.shape

    def body(centre_ref, line_ref, column_ref, wing_ref, strength_ref, widths_ref, out_ref,
             c_ref, l_ref, f_ref, g_ref, power_ref, width_ref, sems):
        copies = [pltpu.make_async_copy(source, target, sems.at[n]) for n, (source, target) in enumerate(
            ((strength_ref, power_ref), (widths_ref, width_ref), (line_ref, l_ref), (column_ref, f_ref),
             (centre_ref, c_ref), (wing_ref, g_ref)))]
        for copy in copies:
            copy.start()
        for copy in copies:
            copy.wait()
        line = l_ref[...]
        power = jnp.zeros(line.shape, jnp.float32)
        width = jnp.ones(line.shape, jnp.float32)
        for n in range(strength.shape[0]):
            hit = line == n
            power = jnp.where(hit, power_ref[n], power)
            width = jnp.where(hit, width_ref[n], width)
        out_ref[0:absorbers, :] = c_ref[...].astype(jnp.float32)
        out_ref[absorbers:2 * absorbers, :] = 0.5 * (f_ref[...] * power)
        out_ref[2 * absorbers:3 * absorbers, :] = 1.0 / width
        out_ref[3 * absorbers:4 * absorbers, :] = jnp.broadcast_to(
            g_ref[...].astype(jnp.float32), (absorbers, spectra))

    return pl.pallas_call(
        body, name="lines", in_specs=[HBM] * 6, out_specs=VMEM,
        out_shape=jax.ShapeDtypeStruct((4 * absorbers, spectra), jnp.float32),
        scratch_shapes=[pltpu.VMEM(centres.shape, jnp.int32), pltpu.VMEM(centres.shape, jnp.int32),
                        pltpu.VMEM(centres.shape, jnp.float32), pltpu.VMEM(wing.shape, jnp.int32),
                        pltpu.SMEM(strength.shape, jnp.float32), pltpu.SMEM(widths.shape, jnp.float32),
                        pltpu.SemaphoreType.DMA((6,))],
    )(centres, line_index, column_factor, wing, strength, widths)


def front(n, flux, coeffs_t, basis, own, over_core, over_x, sketch_matrix, residual):
    spectra, pixels = flux.shape
    count = spectra // PARTS
    absorbers = own.shape[0] // 4
    k = sketch_matrix.shape[1]
    mine = slice(n * count, (n + 1) * count)

    def body(flux_hbm, coeffs_hbm, basis_hbm, m_hbm, own_ref, core_ref, x_ref, *refs):
        res_hbm, keep_ref, send_ref, flux_ref, coeffs_ref, basis_ref, m_ref, res_ref, tau_ref, sems = refs[-10:]
        loads = [pltpu.make_async_copy(source, target, sems.at[i]) for i, (source, target) in enumerate(
            ((flux_hbm.at[mine, :], flux_ref), (coeffs_hbm, coeffs_ref), (basis_hbm, basis_ref), (m_hbm, m_ref)))]
        for copy in loads:
            copy.start()
        w = lax.axis_index("wave")
        core = w % 2
        first = (w * pixels).astype(jnp.float32)
        wing_row = own_ref[3 * absorbers:3 * absorbers + 1, mine]

        def depth(ref, start, height):
            at = lax.broadcasted_iota(jnp.int32, (height, count), 0).astype(jnp.float32) + start
            total = None
            for a in range(absorbers):
                centre, amplitude, inverse = (
                    ref[i * absorbers + a:i * absorbers + a + 1, mine] for i in range(3))
                term = bell(at - centre, amplitude, inverse, wing_row)
                total = term if total is None else total + term
            return total

        def chunk(i, _):
            row = pl.multiple_of(i * CHUNK, CHUNK)
            tau_ref[pl.ds(row, CHUNK), :] = depth(own_ref, first + row.astype(jnp.float32), CHUNK)
            return 0

        lax.fori_loop(0, pixels // CHUNK, chunk, 0)
        for ref, before in ((core_ref, core == 1), (x_ref, core == 0)):
            row = pl.multiple_of(jnp.where(before, 0, pixels - WING), WING)
            tau_ref[pl.ds(row, WING), :] += depth(ref, first + row.astype(jnp.float32), WING)
        for copy in loads[:3]:
            copy.wait()
        for i in range(pixels // T):
            lanes = slice(i * T, (i + 1) * T)
            seen = jnp.exp(-tau_ref[lanes, :].T)
            continuum = lax.dot_general(coeffs_ref[:, mine], basis_ref[:, lanes], (((0,), (0,)), ((), ())),
                                        preferred_element_type=jnp.float32)
            res_ref[:, lanes] = (flux_ref[:, lanes].astype(jnp.float32) - continuum * seen).astype(jnp.bfloat16)
        store = pltpu.make_async_copy(res_ref, res_hbm.at[mine, :], sems.at[4])
        store.start()
        loads[3].wait()
        half = count // 2
        for out, side in ((send_ref, 1 - core), (keep_ref, core)):
            row = pl.multiple_of(side * half, half)
            out[...] = jnp.dot(res_ref[pl.ds(row, half), :], m_ref[...], preferred_element_type=jnp.float32)
        store.wait()

    rows = jax.ShapeDtypeStruct((count // 2, k), jnp.float32)
    earlier = [] if residual is None else [residual]
    return pl.pallas_call(
        body, name="front", in_specs=[HBM] * 4 + [VMEM] * 3 + [HBM] * len(earlier), out_specs=[HBM, VMEM, VMEM],
        out_shape=[jax.ShapeDtypeStruct(flux.shape, jnp.bfloat16), rows, rows],
        input_output_aliases={7: 0} if earlier else {},
        scratch_shapes=[pltpu.VMEM((count, pixels), flux.dtype)]
        + [pltpu.VMEM(a.shape, a.dtype) for a in (coeffs_t, basis, sketch_matrix)]
        + [pltpu.VMEM((count, pixels), jnp.bfloat16), pltpu.VMEM((pixels, count), jnp.float32),
           pltpu.SemaphoreType.DMA((5,))],
        cost_estimate=pl.CostEstimate(flops=2 * count * pixels * k, transcendentals=0,
                                      bytes_accessed=4 * count * pixels + 2 * pixels * k),
        compiler_params=pltpu.CompilerParams(vmem_limit_bytes=FRONT_VMEM),
    )(flux, coeffs_t, basis, sketch_matrix, own, over_core, over_x, *earlier)


def shards(
    observed_flux,
    continuum_coeffs,
    continuum_basis,
    centres,
    line_index,
    column_factor,
    wing_width,
    line_strength,
    line_widths,
    sketch_matrix,
):
    waves = lax.axis_size("wave")
    own = line_table(centres.T, line_index.T, column_factor.T, wing_width[None, :], line_strength, line_widths)
    across = [(i, (i + 1 if i % 2 else i - 1) % waves) for i in range(waves)]
    over_x = lax.ppermute(own, "wave", across)
    over_core = swap(own, "wave", 1)
    here = jnp.maximum(own, 0.0)
    residual, keep, send = None, [], []
    for n in range(PARTS):
        residual, stays, goes = front(n, observed_flux, continuum_coeffs.T, continuum_basis, here,
                                      over_core, over_x, sketch_matrix, residual)
        keep.append(stays)
        send.append(goes)
    return (residual, reduce_and_factor(keep, send, observed_flux.shape[0] * lax.axis_size("spec")))


def solution(mesh):
    return jax.shard_map(
        shards,
        mesh=mesh,
        in_specs=(
            P("spec", "wave"),
            P("spec", None),
            P(None, "wave"),
            P("spec", "wave"),
            P("spec", "wave"),
            P("spec", "wave"),
            P("spec"),
            P(),
            P(),
            P("wave", None),
        ),
        out_specs=(P("spec", "wave"), P()),
        check_vma=False,
    )
```

```python
import jax
import jax.numpy as jnp
from jax import lax
from jax.experimental import pallas as pl
from jax.experimental.pallas import tpu as pltpu
from jax.sharding import PartitionSpec as P

WING = 32
T = 128
S = 8
HI = lax.Precision.HIGHEST

def rows_of(x, k):
    return jnp.broadcast_to(x[k:k + 1, :], x.shape)

def lanes_of(x, c):
    return jnp.broadcast_to(x[:, c:c + 1], x.shape)

NEAR = 2

def split3(x):
    a = x.astype(jnp.bfloat16)
    r = x - a.astype(jnp.float32)
    b = r.astype(jnp.bfloat16)
    return a, b, (r - b.astype(jnp.float32)).astype(jnp.bfloat16)

LEFT, RIGHT = (0, 0, 1, 0, 1, 2), (0, 1, 0, 2, 1, 0)

def stack(parts, order, axis):
    return jnp.concatenate([parts[n] for n in order], axis=axis)

def outer(x, y):
    return lax.dot_general(stack(split3(x), LEFT, 0), stack(split3(y), RIGHT, 0), (((0,), (0,)), ((), ())), preferred_element_type=jnp.float32)

def factor_block(d_ref, x_ref):
    steps = T // S
    sub = lax.broadcasted_iota(jnp.int32, (S, T), 0)
    lane = lax.broadcasted_iota(jnp.int32, (S, T), 1)
    at = [sub == k for k in range(S)]
    D = [d_ref[S * g:S * g + S, 0:T] for g in range(steps)]
    C = [lanes_of(D[0], k) for k in range(S)]
    later = None
    for s in range(steps):
        done = (lane >= S * s) & (lane < S * s + S)
        rows = D[s]
        start = jnp.where(done, jnp.where(lane == sub + S * s, 1.0, 0.0), rows)
        W = [rows_of(start, k) for k in range(S)]
        B = Cn = None
        if s + 1 < steps:
            B = [lanes_of(D[s + 1], S * s + k) for k in range(S)]
            first = list(B)
            Ca = [None] * S
            Cn = [lanes_of(D[s + 1], S * (s + 1) + k) for k in range(S)]
        for k in range(S):
            d = rows_of(C[k], k)
            inv = 1.0 / d
            x_ref[S * s + k:S * s + k + 1, :] = (W[k] * lax.rsqrt(d))[0:1]
            u = {}
            for c in range(k + 1, S):
                u[c] = rows_of(C[c], k) * inv
                C[c] = jnp.where(at[k], u[c], C[c] - C[k] * u[c])
                W[c] = W[c] - u[c] * W[k]
            W[k] = W[k] * inv
            for c in range(k):
                W[c] = W[c] - rows_of(C[k], c) * W[k]
            if B is not None:
                bi = B[k] * inv
                for c in range(k + 1, S):
                    B[c] = B[c] - B[k] * u[c]
                for c in range(S):
                    v = bi * rows_of(B[k], c)
                    Ca[c] = v if k == 0 else Ca[c] + v
        if later is not None:
            for g, part in later:
                D[g] = D[g] - part
        for g in range(s + 1, min(s + 1 + NEAR, steps)):
            raw = first if g == s + 1 else [lanes_of(D[g], S * s + k) for k in range(S)]
            terms = [raw[k] * W[k] for k in range(S)]
            while len(terms) > 1:
                terms = [p + q for p, q in zip(terms[::2], terms[1::2])]
            D[g] = jnp.where(done, 0.0, D[g]) - terms[0]
        later = None
        if s + 1 + NEAR < steps:
            w = W[S - 1]
            for k in range(S - 1):
                w = jnp.where(at[k], W[k], w)
            full = outer(rows, w)
            later = []
            for g in range(s + 1 + NEAR, steps):
                D[g] = jnp.where(done, 0.0, D[g])
                later.append((g, full[S * g:S * g + S, :]))
        C = [p - q for p, q in zip(Cn, Ca)] if Cn is not None else None

def upper_block(b, nb):
    i = jnp.int32(0)
    start = jnp.int32(0)
    for r in range(1, nb):
        first = r * nb - r * (r - 1) // 2
        i = i + (b >= first).astype(jnp.int32)
        start = jnp.where(b >= first, first, start)
    return i, i + b - start


def blocks_of(x, slots, t, nb):
    b = jnp.minimum(x * slots + t, nb * (nb + 1) // 2 - 1)
    i, j = upper_block(b, nb)
    return pl.multiple_of(i * T, T), pl.multiple_of(j * T, T)


def gram_blocks(mine, other, slots, scale):
    part, k = mine[0].shape

    def body(*refs):
        mine_refs, other_refs, (keep_ref, send_ref, s_ref, g_ref) = refs[:PARTS], refs[PARTS:2 * PARTS], refs[2 * PARTS:]
        w = lax.axis_index("wave")
        core, x = w % 2, w // 2
        for n in range(PARTS):
            s_ref[n * part:(n + 1) * part, :] = mine_refs[n][...] + other_refs[n][...]
        for t in range(slots):
            i, j = blocks_of(x, slots, t, k // T)
            g_ref[...] = scale * lax.dot_general(
                s_ref[:, pl.ds(i, T)], s_ref[:, pl.ds(j, T)], (((0,), (0,)), ((), ())),
                precision=HI, preferred_element_type=jnp.float32)
            half = T // 2
            keep_ref[t] = g_ref[pl.ds(pl.multiple_of(core * half, half), half), :]
            send_ref[t] = g_ref[pl.ds(pl.multiple_of((1 - core) * half, half), half), :]

    shape = jax.ShapeDtypeStruct((slots, T // 2, T), jnp.float32)
    return pl.pallas_call(
        body, name="gram", out_shape=(shape, shape),
        scratch_shapes=[pltpu.VMEM((PARTS * part, k), jnp.float32), pltpu.VMEM((T, T), jnp.float32)],
        compiler_params=pltpu.CompilerParams(vmem_limit_bytes=32 << 20),
    )(*mine, *other)


def factor(pieces, offsets, slots, n):
    nb = n // T
    part = T // 4

    def body(*refs):
        piece_refs, (r_ref, w_ref, x_ref) = refs[:len(pieces)], refs[len(pieces):]
        w = lax.axis_index("wave")
        y = lax.axis_index("spec") % 2
        blocks = {}
        for ref, (dw, dy) in zip(piece_refs, offsets):
            if dw // 2 not in blocks:
                blocks[dw // 2] = [blocks_of((w // 2) ^ (dw // 2), slots, t, nb) for t in range(slots)]
            row = ((w % 2) ^ (dw % 2)) * (T // 2) + (y ^ dy) * part
            for t, (i, j) in enumerate(blocks[dw // 2]):
                w_ref[pl.ds(pl.multiple_of(i + row, part), part), pl.ds(j, T)] = ref[t]
        for b in range(1, nb):
            r_ref[b * T:(b + 1) * T, 0:b * T] = jnp.zeros((T, b * T), jnp.float32)
        row = lax.broadcasted_iota(jnp.int32, (T, T), 0)
        col = lax.broadcasted_iota(jnp.int32, (T, T), 1)

        for b in range(nb):
            low, high = b * T, (b + 1) * T
            factor_block(w_ref.at[low:high, low:high], x_ref)
            inverse = jnp.where(row >= col, x_ref[...], 0.0)
            rows = jnp.dot(stack(split3(inverse), LEFT, 1), stack(split3(w_ref[low:high, low:n]), RIGHT, 0),
                           preferred_element_type=jnp.float32)
            r_ref[low:high, low:high] = jnp.where(row <= col, rows[:, 0:T], 0.0)
            if b == nb - 1:
                break
            r_ref[low:high, high:n] = rows[:, T:]
            right = stack(split3(rows[:, T:]), RIGHT, 0)
            for i in range(b + 1, nb):
                left = stack(split3(rows[:, (i - b) * T:(i - b + 1) * T].T), LEFT, 1)
                w_ref[i * T:(i + 1) * T, i * T:n] -= jnp.dot(
                    left, right[:, (i - b - 1) * T:], preferred_element_type=jnp.float32)

    return pl.pallas_call(
        body, name="factor", out_shape=jax.ShapeDtypeStruct((n, n), jnp.float32),
        scratch_shapes=[pltpu.VMEM((n, n), jnp.float32), pltpu.VMEM((T, T), jnp.float32)],
        compiler_params=pltpu.CompilerParams(vmem_limit_bytes=32 << 20),
    )(*pieces)


def swap(x, axis, bit):
    return lax.ppermute(x, axis, [(i, i ^ bit) for i in range(lax.axis_size(axis))])


def bits_from(first, count):
    bits = []
    while first < count:
        bits.append(first)
        first *= 2
    return bits


def half_of(x, which, dim):
    size = x.shape[dim] // 2
    return lax.dynamic_slice_in_dim(x, which * size, size, dim)


def reduce_and_factor(mine, send, spectra_total):
    waves, specs = lax.axis_size("wave"), lax.axis_size("spec")
    y = lax.axis_index("spec") % 2
    k = mine[0].shape[1]
    slots = -(-((k // T) * (k // T + 1) // 2) // (waves // 2))
    other = [swap(p, "wave", 1) for p in send]
    for bit in bits_from(2, waves):
        mine = [p + q for p, q in zip(mine, other)]
        other = [swap(p, "wave", bit) for p in mine]
    keep, send = gram_blocks(mine, other, slots, 1.0 / spectra_total)
    got = swap(send, "wave", 1)
    mine = half_of(keep, y, 1) + half_of(got, y, 1)
    other = half_of(keep, 1 - y, 1) + half_of(got, 1 - y, 1)
    mine = mine + swap(other, "spec", 1)
    for bit in bits_from(2, specs):
        mine = mine + swap(mine, "spec", bit)
    pieces, offsets = [mine], [(0, 0)]
    steps = [("spec", 1)] + [("wave", b) for b in bits_from(2, waves)] + [("wave", 1)]
    for axis, bit in steps:
        pieces = pieces + [swap(p, axis, bit) for p in pieces]
        offsets = offsets + [(w ^ (bit if axis == "wave" else 0), y_ ^ (bit if axis == "spec" else 0)) for w, y_ in offsets]
    return factor(pieces, offsets, slots, k)


CHUNK = 32


def bell(offset, half_amplitude, inverse_width, wing):
    u = offset * inverse_width
    square = u * u
    height = jnp.where(jnp.abs(offset) <= wing, half_amplitude, 0.0)
    return height, 1.0 + square, height * jnp.exp2(-square)


def summed(bells):
    total = sum(b[2] for b in bells[1:]) + bells[0][2]
    for (p, q, _), (r, s, _) in zip(bells[::2], bells[1::2]):
        total = total + (p * s + r * q) / (q * s)
    if len(bells) % 2:
        total = total + bells[-1][0] / bells[-1][1]
    return total


PARTS = 2
FRONT_VMEM = 107 << 19
SMEM = pl.BlockSpec(memory_space=pltpu.SMEM)
VMEM = pl.BlockSpec(memory_space=pltpu.VMEM)
HBM = pl.BlockSpec(memory_space=pltpu.HBM)


def line_table(centres, line_index, column_factor, wing, strength, widths):
    absorbers, spectra = centres.shape

    def body(centre_ref, line_ref, column_ref, wing_ref, strength_ref, widths_ref, out_ref,
             c_ref, l_ref, f_ref, g_ref, power_ref, width_ref, sems):
        copies = [pltpu.make_async_copy(source, target, sems.at[n]) for n, (source, target) in enumerate(
            ((strength_ref, power_ref), (widths_ref, width_ref), (line_ref, l_ref), (column_ref, f_ref),
             (centre_ref, c_ref), (wing_ref, g_ref)))]
        for copy in copies:
            copy.start()
        for copy in copies:
            copy.wait()
        line = l_ref[...]
        power = jnp.zeros(line.shape, jnp.float32)
        width = jnp.ones(line.shape, jnp.float32)
        for n in range(strength.shape[0]):
            hit = line == n
            power = jnp.where(hit, power_ref[n], power)
            width = jnp.where(hit, width_ref[n], width)
        out_ref[0:absorbers, :] = c_ref[...].astype(jnp.float32)
        out_ref[absorbers:2 * absorbers, :] = 0.5 * (f_ref[...] * power)
        out_ref[2 * absorbers:3 * absorbers, :] = 1.0 / width
        out_ref[3 * absorbers:4 * absorbers, :] = jnp.broadcast_to(
            g_ref[...].astype(jnp.float32), (absorbers, spectra))

    return pl.pallas_call(
        body, name="lines", in_specs=[HBM] * 6, out_specs=VMEM,
        out_shape=jax.ShapeDtypeStruct((4 * absorbers, spectra), jnp.float32),
        scratch_shapes=[pltpu.VMEM(centres.shape, jnp.int32), pltpu.VMEM(centres.shape, jnp.int32),
                        pltpu.VMEM(centres.shape, jnp.float32), pltpu.VMEM(wing.shape, jnp.int32),
                        pltpu.SMEM(strength.shape, jnp.float32), pltpu.SMEM(widths.shape, jnp.float32),
                        pltpu.SemaphoreType.DMA((6,))],
    )(centres, line_index, column_factor, wing, strength, widths)


def front(n, flux, coeffs_t, basis, own, over_core, over_x, sketch_matrix, residual):
    spectra, pixels = flux.shape
    count = spectra // PARTS
    absorbers = own.shape[0] // 4
    k = sketch_matrix.shape[1]
    mine = slice(n * count, (n + 1) * count)

    def body(flux_hbm, coeffs_hbm, basis_hbm, m_hbm, own_ref, core_ref, x_ref, *refs):
        res_hbm, keep_ref, send_ref, flux_ref, coeffs_ref, basis_ref, m_ref, res_ref, tau_ref, sems = refs[-10:]
        loads = [pltpu.make_async_copy(source, target, sems.at[i]) for i, (source, target) in enumerate(
            ((flux_hbm.at[mine, :], flux_ref), (coeffs_hbm, coeffs_ref), (basis_hbm, basis_ref), (m_hbm, m_ref)))]
        for copy in loads:
            copy.start()
        w = lax.axis_index("wave")
        core = w % 2
        first = (w * pixels).astype(jnp.float32)
        wing_row = own_ref[3 * absorbers:3 * absorbers + 1, mine]

        def depth(ref, start, height):
            at = lax.broadcasted_iota(jnp.int32, (height, count), 0).astype(jnp.float32) + start
            bells = []
            for a in range(absorbers):
                centre, amplitude, inverse = (
                    ref[i * absorbers + a:i * absorbers + a + 1, mine] for i in range(3))
                bells.append(bell(at - centre, amplitude, inverse, wing_row))
            return summed(bells)

        def chunk(i, _):
            row = pl.multiple_of(i * CHUNK, CHUNK)
            tau_ref[pl.ds(row, CHUNK), :] = depth(own_ref, first + row.astype(jnp.float32), CHUNK)
            return 0

        lax.fori_loop(0, pixels // CHUNK, chunk, 0)
        for ref, before in ((core_ref, core == 1), (x_ref, core == 0)):
            row = pl.multiple_of(jnp.where(before, 0, pixels - WING), WING)
            tau_ref[pl.ds(row, WING), :] += depth(ref, first + row.astype(jnp.float32), WING)
        for copy in loads[:3]:
            copy.wait()
        for i in range(pixels // T):
            lanes = slice(i * T, (i + 1) * T)
            seen = jnp.exp(-tau_ref[lanes, :].T)
            continuum = lax.dot_general(coeffs_ref[:, mine], basis_ref[:, lanes], (((0,), (0,)), ((), ())),
                                        preferred_element_type=jnp.float32)
            res_ref[:, lanes] = (flux_ref[:, lanes].astype(jnp.float32) - continuum * seen).astype(jnp.bfloat16)
        store = pltpu.make_async_copy(res_ref, res_hbm.at[mine, :], sems.at[4])
        store.start()
        loads[3].wait()
        half = count // 2
        for out, side in ((send_ref, 1 - core), (keep_ref, core)):
            row = pl.multiple_of(side * half, half)
            out[...] = jnp.dot(res_ref[pl.ds(row, half), :], m_ref[...], preferred_element_type=jnp.float32)
        store.wait()

    rows = jax.ShapeDtypeStruct((count // 2, k), jnp.float32)
    earlier = [] if residual is None else [residual]
    return pl.pallas_call(
        body, name="front", in_specs=[HBM] * 4 + [VMEM] * 3 + [HBM] * len(earlier), out_specs=[HBM, VMEM, VMEM],
        out_shape=[jax.ShapeDtypeStruct(flux.shape, jnp.bfloat16), rows, rows],
        input_output_aliases={7: 0} if earlier else {},
        scratch_shapes=[pltpu.VMEM((count, pixels), flux.dtype)]
        + [pltpu.VMEM(a.shape, a.dtype) for a in (coeffs_t, basis, sketch_matrix)]
        + [pltpu.VMEM((count, pixels), jnp.bfloat16), pltpu.VMEM((pixels, count), jnp.float32),
           pltpu.SemaphoreType.DMA((5,))],
        cost_estimate=pl.CostEstimate(flops=2 * count * pixels * k, transcendentals=0,
                                      bytes_accessed=4 * count * pixels + 2 * pixels * k),
        compiler_params=pltpu.CompilerParams(vmem_limit_bytes=FRONT_VMEM),
    )(flux, coeffs_t, basis, sketch_matrix, own, over_core, over_x, *earlier)


def shards(
    observed_flux,
    continuum_coeffs,
    continuum_basis,
    centres,
    line_index,
    column_factor,
    wing_width,
    line_strength,
    line_widths,
    sketch_matrix,
):
    waves = lax.axis_size("wave")
    own = line_table(centres.T, line_index.T, column_factor.T, wing_width[None, :], line_strength, line_widths)
    across = [(i, (i + 1 if i % 2 else i - 1) % waves) for i in range(waves)]
    over_x = lax.ppermute(own, "wave", across)
    over_core = swap(own, "wave", 1)
    here = jnp.maximum(own, 0.0)
    residual, keep, send = None, [], []
    for n in range(PARTS):
        residual, stays, goes = front(n, observed_flux, continuum_coeffs.T, continuum_basis, here,
                                      over_core, over_x, sketch_matrix, residual)
        keep.append(stays)
        send.append(goes)
    return (residual, reduce_and_factor(keep, send, observed_flux.shape[0] * lax.axis_size("spec")))


def solution(mesh):
    return jax.shard_map(
        shards,
        mesh=mesh,
        in_specs=(
            P("spec", "wave"),
            P("spec", None),
            P(None, "wave"),
            P("spec", "wave"),
            P("spec", "wave"),
            P("spec", "wave"),
            P("spec"),
            P(),
            P(),
            P("wave", None),
        ),
        out_specs=(P("spec", "wave"), P()),
        check_vma=False,
    )
```
